256 devices in a mesh: section: 8 (over y, x_hi), ctx: 32 (over x_lo, z, core).
Axes of the slice: x: 4 (x_hi: 2, x_lo: 2; x = x_hi * 2 + x_lo), y: 4, z: 8, core: 2. Of those that a mesh axis runs over, the one named last changes fastest.
Arguments:
- latent_state: bfloat16 [8, 5120, 1536], P('section', 'ctx'), may hold values from -20 to 20
- lead_step: int32 [8], replicated, may hold values from 0 to 7, each once
- tail_qkv: bfloat16 [1536, 1280], P(('section', 'ctx')), may hold values from -0.15625 to 0.15625
- tail_out: bfloat16 [1536, 768], P(('section', 'ctx')), may hold values from -0.21875 to 0.21875
- head_qkv: bfloat16 [1536, 1280], P(('section', 'ctx')), may hold values from -0.15625 to 0.15625
- head_out: bfloat16 [1536, 768], P(('section', 'ctx')), may hold values from -0.21875 to 0.21875
- modulation: float32 [2, 2, 9, 1536], replicated, may hold values from 0.5 to 1.5
- qk_gain: float32 [2, 2, 128], replicated, may hold values from 1 to 2
Outputs:
- tail_state: bfloat16 [8, 5120, 1536], P('section', 'ctx')
- head_state: bfloat16 [8, 5120, 1536], P('section', 'ctx')
The draws below stay inside these ranges and needn't reach their ends.
Inputs may be any that keep to these rules, and one draw needn't show every extreme that they name: `lead_step`: every section holds a different lead time.
All inputs are finite; a program needn't handle non-finite values.
Results may differ from the reference program's by a relative error of at most 0.01.
Values may be sent and summed in bfloat16 or wider, within the bound.
No kernel may reach another device: no remote copies, remote signals or barrier semaphores. Data moves between devices by JAX's collectives and lax.ppermute only.
A program may use at most 64 MiB of HBM per device.

```python
import math
import jax
import jax.numpy as jnp
from jax import lax

D = 1536
QH = 6
KVH = 2
HD = 128
QW = 768
KW = 256
SEQ = 5120
LEADS = 9
N_SECTION = 8
N_CTX = 32


def draw_latent_state(key, part):
    subkeys = jax.random.split(key, 3)
    row_scale = jnp.exp(jax.random.uniform(subkeys[0], (N_SECTION, SEQ, 1), jnp.float32, math.log(0.3), math.log(3.0)))
    col_scale = jnp.exp(jax.random.uniform(subkeys[1], (1, 1, D), jnp.float32, math.log(0.3), math.log(3.0)))
    values = jnp.clip(jax.random.normal(subkeys[2], (N_SECTION, SEQ, D), jnp.float32), -3.0, 3.0)
    return (0.5 * row_scale * col_scale * values).astype(jnp.bfloat16)


def block_scale(stream_key, dims, shards, least, high):
    def one(position, blocks):
        heights = jax.random.uniform(jax.random.fold_in(jax.random.fold_in(stream_key, 6), position), (blocks,), jnp.float32, least / len(shards), high / len(shards))
        return jnp.repeat(jnp.exp(heights), dims[position] // blocks).reshape((-1,) + (1,) * (len(dims) - position - 1))

    level = one(*shards[0])
    for cut in shards[1:]:
        level = level * one(*cut)
    return level


def normal_values(stream_key, shape, spread, bound, cuts=(), held_as=jnp.bfloat16):
    level = block_scale(stream_key, shape, cuts, -0.22, 0.18) if cuts else 1.0
    entries = jax.random.normal(stream_key, shape, jnp.float32) * spread * level
    return jnp.minimum(jnp.maximum(entries, -bound), bound).astype(held_as)


def setup_inputs(seed: int = 0) -> dict:
    key_list = jax.random.split(jax.random.key(seed), 9)
    return {
        "latent_state": draw_latent_state(jax.random.fold_in(key_list[8], 71), 0),
        "lead_step": jax.random.permutation(key_list[1], N_SECTION).astype(jnp.int32),
        "tail_qkv": normal_values(key_list[2], (D, QW + 2 * KW), D ** -0.5, 0.15625, ((0, 256),)),
        "tail_out": normal_values(key_list[3], (D, QW), QW ** -0.5, 0.21875, ((0, 256),)),
        "head_qkv": normal_values(key_list[4], (D, QW + 2 * KW), D ** -0.5, 0.15625, ((0, 256),)),
        "head_out": normal_values(key_list[5], (D, QW), QW ** -0.5, 0.21875, ((0, 256),)),
        "modulation": jnp.clip(1.0 + 0.1 * jax.random.normal(key_list[6], (2, 2, LEADS, D), jnp.float32), 0.5, 1.5),
        "qk_gain": jnp.clip(jnp.exp(jax.random.uniform(key_list[7], (2, 2, HD), jnp.float32, math.log(1.0), math.log(2.0))), 1.0, 2.0),
    }


def qk_normal(values, gain_row):
    factor = lax.rsqrt(lax.optimization_barrier(jnp.mean(values * values, axis=-1, keepdims=True)) + 1e-06)
    return (values * factor * gain_row).astype(jnp.bfloat16)

def attention_layer(inputs, w_joined, w_output, norm_gain, res_gate, q_gain, k_gain):
    seq_len = inputs.shape[0]
    groups = QH // KVH
    widened = inputs.astype(jnp.float32)
    factor = lax.rsqrt(lax.optimization_barrier(jnp.mean(widened * widened, axis=-1, keepdims=True)) + 1e-06)
    normed = (widened * factor * norm_gain).astype(jnp.bfloat16)
    projected = jnp.dot(normed, w_joined, preferred_element_type=jnp.float32)
    queries = qk_normal(projected[:, :QH * HD].reshape(seq_len, KVH, groups, HD), q_gain)
    key_rows = qk_normal(projected[:, QH * HD:(QH + KVH) * HD].reshape(seq_len, KVH, HD), k_gain)
    val_rows = projected[:, (QH + KVH) * HD:].astype(jnp.bfloat16).reshape(seq_len, KVH, HD)
    key_wide = lax.optimization_barrier(key_rows).astype(jnp.float32)
    val_wide = lax.optimization_barrier(val_rows).astype(jnp.float32)
    query_blocks = queries.reshape(N_CTX, seq_len // N_CTX, KVH, groups, HD)
    score_scale = float(HD) ** (-0.5)

    def per_block(query_block):
        query_wide = lax.optimization_barrier(query_block).astype(jnp.float32)
        scores = jnp.einsum('tkgd,skd->tkgs', query_wide, key_wide) * score_scale
        weights = jnp.exp(scores)
        denominator = lax.optimization_barrier(jnp.sum(weights, axis=-1))
        rounded = lax.optimization_barrier(weights.astype(jnp.bfloat16)).astype(jnp.float32)
        numerator = jnp.einsum('tkgs,skd->tkgd', rounded, val_wide)
        return (numerator / denominator[..., None]).astype(jnp.bfloat16)
    attended = lax.map(per_block, query_blocks).reshape(seq_len, QH * HD)
    update = jnp.dot(attended, w_output.T, preferred_element_type=jnp.float32)
    return (widened + res_gate * update).astype(jnp.bfloat16)

def reference(latent_state, lead_step, tail_qkv, tail_out, head_qkv, head_out, modulation, qk_gain):
    section_count = latent_state.shape[0]
    tails = []
    for section_pos in range(section_count):
        lead_now = lead_step[section_pos]
        tails.append(attention_layer(latent_state[section_pos], tail_qkv, tail_out, modulation[0, 0, lead_now], modulation[0, 1, lead_now], qk_gain[0, 0], qk_gain[0, 1]))
    heads = []
    for section_pos in range(section_count):
        sender = (section_pos - 1) % section_count
        lead_next = lead_step[sender] + 1
        heads.append(attention_layer(tails[sender], head_qkv, head_out, modulation[1, 0, lead_next], modulation[1, 1, lead_next], qk_gain[1, 0], qk_gain[1, 1]))
    return (jnp.stack(tails), jnp.stack(heads))
```

```python
import functools
import math

import jax
import jax.numpy as jnp
from jax import lax
from jax.experimental import pallas as pl
from jax.experimental.pallas import tpu as pltpu
from jax.sharding import PartitionSpec as P

D = 1536
HD = 128
GH = 3
QC = GH * HD
KVC = 2 * HD
AC = KVC + QC
TOK = 160
PAIR = 2 * TOK
NZ = 8
NX = 4
NY = 4
EPS = 1e-06
EXP2_SCALE = math.log2(math.e) * HD ** (-0.5)
VMEM = pl.BlockSpec(memory_space=pltpu.VMEM)
SMEM = pl.BlockSpec(memory_space=pltpu.SMEM)
BF = jnp.bfloat16
F32 = jnp.float32


def flat_id(x, y, z, c):
    return (y * 2 + (x >> 1)) * 32 + (x & 1) * 16 + z * 2 + c


CORE_SWAP = [(i, i ^ 1) for i in range(32)]
X_SWAP = [(i, i ^ 16) for i in range(32)]
ZC_GROUPS = [[xl * 16 + i for i in range(16)] for xl in range(2)]
X_GROUPS = [
    [flat_id(x, y, z, c) for x in range(NX)] for y in range(NY) for z in range(NZ) for c in range(2)
]
Y_GROUPS = [[y * 2 + xh for y in range(NY)] for xh in range(2)]
BOTH = ("section", "ctx")


def z_step(by):
    return [(i, (i & 16) | ((((i >> 1) + by) % NZ) << 1) | (i & 1)) for i in range(32)]


def x_step(by):
    return [
        (flat_id(x, y, z, c), flat_id((x + by) % NX, y, z, c))
        for x in range(NX) for y in range(NY) for z in range(NZ) for c in range(2)
    ]


def y_step(by):
    return [(i, (((i >> 1) + by) % NY) << 1 | (i & 1)) for i in range(8)]


def section_step(by):
    return [(s, (s + by) % 8) for s in range(8)]


def cost(flops, nbytes, trans=0):
    return pl.CostEstimate(flops=int(flops), bytes_accessed=int(nbytes), transcendentals=int(trans))


def params():
    return pltpu.CompilerParams(vmem_limit_bytes=16 * 1024 * 1024)


def head_normal(values, gain_row):
    factor = lax.rsqrt(jnp.mean(values * values, axis=-1, keepdims=True) + EPS)
    return (values * factor * gain_row).astype(BF)


def project_body(layer, lead_ref, own_ref, oth_ref, wkv_ref, wq_ref, mod_ref, gain_ref, kv_ref, q_ref, normed):
    row = mod_ref[layer, 0, pl.ds(lead_ref[0] + layer, 1), :]
    for part, ref in enumerate((own_ref, oth_ref)):
        x = ref[...].astype(F32)
        factor = lax.rsqrt(jnp.mean(x * x, axis=-1, keepdims=True) + EPS)
        normed[part * TOK : (part + 1) * TOK, :] = (x * factor * row).astype(BF)
    kv = jnp.dot(normed[...], wkv_ref[...], preferred_element_type=F32)
    kv_ref[:, :HD] = head_normal(kv[:, :HD], gain_ref[layer, 1:2, :])
    kv_ref[:, HD:] = kv[:, HD:].astype(BF)
    for h in range(GH):
        q = jnp.dot(
            normed[...], wq_ref[:, h * HD : (h + 1) * HD], preferred_element_type=F32
        )
        q_ref[h] = head_normal(q, gain_ref[layer, 0:1, :])


def project(layer, lead, own, oth, wkv, wq, modulation, qk_gain):
    return pl.pallas_call(
        functools.partial(project_body, layer),
        out_shape=(
            jax.ShapeDtypeStruct((PAIR, KVC), BF),
            jax.ShapeDtypeStruct((GH, PAIR, HD), BF),
        ),
        in_specs=[SMEM] + [VMEM] * 6,
        out_specs=(VMEM, VMEM),
        scratch_shapes=[pltpu.VMEM((PAIR, D), BF)],
        compiler_params=params(),
        cost_estimate=cost(2 * PAIR * D * AC, 4 * 1024 * 1024),
        name="project",
    )(lead, own, oth, wkv, wq, modulation, qk_gain)


def add_keys(q, keys, vals):
    scores = lax.dot_general(q, keys, (((1,), (1,)), ((), ())), preferred_element_type=F32)
    weights = jnp.exp2(scores * EXP2_SCALE)
    return (
        jnp.dot(weights.astype(BF), vals, preferred_element_type=F32),
        jnp.sum(weights, axis=-1, keepdims=True),
    )


def attend_body(first, n_chunks, *refs):
    q_own, q_par = refs[:2]
    chunks = refs[2 : 2 + n_chunks]
    rest = refs[2 + n_chunks :]
    if first:
        num_out, den_out = rest
    else:
        num_in, den_in, num_out, den_out = rest
    def one_head(h, carry):
        for side, q_ref in enumerate((q_own, q_par)):
            q = q_ref[h]
            num = den = None
            for ref in chunks:
                part, total = add_keys(q, ref[:, :HD], ref[:, HD:])
                num = part if num is None else num + part
                den = total if den is None else den + total
            den = jnp.broadcast_to(den, (PAIR, HD))
            if not first:
                num = num + num_in[side, h]
                den = den + den_in[side, h]
            num_out[side, h] = num
            den_out[side, h] = den
        return carry

    lax.fori_loop(0, GH, one_head, 0)


def attend(q_own, q_par, chunks, state=None):
    shape = jax.ShapeDtypeStruct((2, GH, PAIR, HD), F32)
    first = state is None
    n = len(chunks)
    return pl.pallas_call(
        functools.partial(attend_body, first, n),
        out_shape=(shape, shape),
        in_specs=[VMEM] * (2 + n + (0 if first else 2)),
        out_specs=(VMEM, VMEM),
        input_output_aliases={} if first else {2 + n: 0, 3 + n: 1},
        compiler_params=params(),
        cost_estimate=cost(
            2 * GH * PAIR * PAIR * n * HD * 4, 2 * 1024 * 1024, 2 * GH * PAIR * PAIR * n
        ),
        name="attend",
    )(q_own, q_par, *chunks, *(() if first else state))


def last_body(q_own, q_par, chunk, num_in, den_in, num_out, den_out, msg):
    keys, vals = chunk[:, :HD], chunk[:, HD:]
    lane = lax.broadcasted_iota(jnp.int32, (PAIR, HD), 1)
    plane = jnp.zeros((PAIR, HD), F32)
    for h in range(GH):
        num, den = add_keys(q_par[h], keys, vals)
        msg[h] = (num + num_in[1, h]).astype(BF)
        den = jnp.broadcast_to(den, (PAIR, HD)) + den_in[1, h]
        high = den.astype(BF).astype(F32)
        plane = jnp.where(lane == 2 * h, high, plane)
        plane = jnp.where(lane == 2 * h + 1, den - high, plane)
    msg[GH] = plane.astype(BF)
    for h in range(GH):
        num, den = add_keys(q_own[h], keys, vals)
        num_out[h] = num + num_in[0, h]
        den_out[h] = jnp.broadcast_to(den, (PAIR, HD)) + den_in[0, h]


def attend_last(q_own, q_par, chunk, state):
    shape = jax.ShapeDtypeStruct((GH, PAIR, HD), F32)
    return pl.pallas_call(
        last_body,
        out_shape=(shape, shape, jax.ShapeDtypeStruct((GH + 1, PAIR, HD), BF)),
        in_specs=[VMEM] * 5,
        out_specs=(VMEM,) * 3,
        compiler_params=params(),
        cost_estimate=cost(
            2 * GH * PAIR * PAIR * HD * 4, 2 * 1024 * 1024, 2 * GH * PAIR * PAIR
        ),
        name="attend_last",
    )(q_own, q_par, chunk, *state)


def merge_body(num_ref, den_ref, msg, out_own, out_oth):
    plane = msg[GH].astype(F32)
    for h in range(GH):
        den = den_ref[h][:, :1] + plane[:, 2 * h : 2 * h + 1] + plane[:, 2 * h + 1 : 2 * h + 2]
        value = ((num_ref[h] + msg[h].astype(F32)) / den).astype(BF)
        out_own[:, h * HD : (h + 1) * HD] = value[:TOK]
        out_oth[:, h * HD : (h + 1) * HD] = value[TOK:]


def merge(num, den, msg):
    shape = jax.ShapeDtypeStruct((TOK, QC), BF)
    return pl.pallas_call(
        merge_body,
        out_shape=(shape, shape),
        in_specs=[VMEM] * 3,
        out_specs=(VMEM, VMEM),
        compiler_params=params(),
        cost_estimate=cost(GH * PAIR * HD * 4, 1024 * 1024),
        name="merge",
    )(num, den, msg)


def output_body(layer, n, lead_ref, *refs):
    att, x, (w_own, w_oth, mod_ref), outs = (
        refs[: 2 * n],
        refs[2 * n : 3 * n],
        refs[3 * n : 3 * n + 3],
        refs[3 * n + 3 :],
    )
    gate = mod_ref[layer, 1, pl.ds(lead_ref[0] + layer, 1), :]
    dims = (((1,), (1,)), ((), ()))
    for part in range(n):
        update = lax.dot_general(att[2 * part][...], w_own[...], dims, preferred_element_type=F32)
        update += lax.dot_general(
            att[2 * part + 1][...], w_oth[...], dims, preferred_element_type=F32
        )
        outs[part][...] = (x[part][...].astype(F32) + gate * update).astype(BF)


def output(layer, lead, att, x, w_own, w_oth, modulation):
    n = len(x)
    shape = jax.ShapeDtypeStruct((TOK, D), BF)
    out = pl.pallas_call(
        functools.partial(output_body, layer, n),
        out_shape=(shape,) * n,
        in_specs=[SMEM] + [VMEM] * (3 * n + 3),
        out_specs=(VMEM,) * n,
        compiler_params=params(),
        cost_estimate=cost(2 * n * TOK * D * 2 * QC, 4 * 1024 * 1024),
        name="output",
    )(lead, *att, *x, w_own, w_oth, modulation)
    return out


def after(value, *events):
    return lax.optimization_barrier((value, *events))[0]


def attention(kv, q, tick=lambda k, event: None):
    q_par = lax.ppermute(q, "ctx", X_SWAP)
    up = lax.ppermute(kv, "ctx", z_step(1))
    down = lax.ppermute(kv, "ctx", z_step(-1))
    tick(0, up)
    state = attend(q, q_par, (kv,))
    for k in range(2):
        next_up = lax.ppermute(up, "ctx", z_step(1))
        next_down = lax.ppermute(down, "ctx", z_step(-1))
        state = attend(q, q_par, (up, down), state)
        up, down, state = lax.optimization_barrier((next_up, next_down, state))
        tick(k + 1, up)
    far = lax.ppermute(up, "ctx", z_step(1))
    state = attend(q, q_par, (up, down), state)
    num, den, msg = attend_last(q, q_par, far, state)
    msg = lax.ppermute(msg, "ctx", X_SWAP)
    return merge(num, den, msg)


def assemble_body(tail_qkv, tail_out, head_qkv, head_out, now_ref, later_ref):
    nq, nk = 2 * QC, 2 * HD
    for c in range(2):

        def qkv(ref):
            return (
                ref[:, nq + c * HD : nq + (c + 1) * HD],
                ref[:, nq + nk + c * HD : nq + nk + (c + 1) * HD],
                ref[:, c * QC : (c + 1) * QC],
            )

        first = jnp.concatenate(qkv(tail_qkv), axis=1)
        second = jnp.concatenate(
            (tail_out[:, c * QC : (c + 1) * QC], *qkv(head_qkv), head_out[:, c * QC : (c + 1) * QC]),
            axis=1,
        )
        for z in range(NZ):
            now_ref[2 * z + c] = first
            later_ref[2 * z + c] = second


def assemble(tail_qkv, tail_out, head_qkv, head_out):
    rows = tail_qkv.shape[0]
    return pl.pallas_call(
        assemble_body,
        out_shape=(
            jax.ShapeDtypeStruct((2 * NZ, rows, AC), BF),
            jax.ShapeDtypeStruct((2 * NZ, rows, AC + 2 * QC), BF),
        ),
        in_specs=[VMEM] * 4,
        out_specs=(VMEM, VMEM),
        compiler_params=params(),
        cost_estimate=cost(0, 1024 * 1024),
        name="assemble",
    )(tail_qkv, tail_out, head_qkv, head_out)


def gather(rows, axis, groups):
    n = len(groups[0])
    spread = jnp.broadcast_to(rows[None], (n, *rows.shape))
    got = lax.all_to_all(spread, axis, 0, 0, axis_index_groups=groups)
    return got.reshape(n * rows.shape[0], rows.shape[1])


def place_body(n_sets, pos_ref, *refs):
    for k in range(n_sets):
        pieces, out = refs[4 * k : 4 * k + 4], refs[4 * n_sets + k]
        at = pos_ref[k]
        for ref, back in zip(pieces, (0, 1, 3, 2)):
            out[lax.rem(at + 4 - back, 4)] = ref[...]


def place(positions, sets):
    shapes = [jax.ShapeDtypeStruct((4, *pieces[0].shape), BF) for pieces in sets]
    return pl.pallas_call(
        functools.partial(place_body, len(sets)),
        out_shape=tuple(shapes),
        in_specs=[SMEM] + [VMEM] * (4 * len(sets)),
        out_specs=(VMEM,) * len(sets),
        compiler_params=params(),
        cost_estimate=cost(0, sum(8 * p[0].size for p in sets)),
        name="place",
    )(positions, *[p for pieces in sets for p in pieces])


def ring_of_4(rows, axis, step):
    return (rows, *(lax.ppermute(rows, axis, step(by)) for by in (1, -1, 2)))


def gather_x(rows):
    return gather(rows, BOTH, X_GROUPS)


def gather_y(rows):
    return gather(rows, "section", Y_GROUPS)


def per_device(
    latent_state, lead_step, tail_qkv, tail_out, head_qkv, head_out, modulation, qk_gain
):
    section_pos = lax.axis_index("section")
    section_count = lax.axis_size("section")
    sender = jnp.mod(section_pos - 1 + section_count, section_count)
    lead = lax.dynamic_slice(lead_step, (sender,), (1,))
    x_own = lax.ppermute(latent_state[0], "section", section_step(1))

    now, rest = assemble(tail_qkv, tail_out, head_qkv, head_out)
    now = lax.all_to_all(now, "ctx", 0, 0, axis_index_groups=ZC_GROUPS).reshape(-1, AC)
    now, x_own = lax.optimization_barrier((now, x_own))
    kv_w, q_w, rest = lax.optimization_barrier((now[:, :KVC], now[:, KVC:], rest))
    rest = lax.all_to_all(rest, "ctx", 0, 0, axis_index_groups=ZC_GROUPS)
    y_pos = section_pos // 2
    x_pos = (section_pos % 2) * 2 + lax.axis_index("ctx") // 16
    kv_w, q_w = place(
        jnp.stack([y_pos, x_pos]),
        (ring_of_4(kv_w, "section", y_step), ring_of_4(q_w, BOTH, x_step)),
    )
    kv_w, q_w = place(
        jnp.stack([x_pos, y_pos]),
        (
            ring_of_4(kv_w.reshape(-1, KVC), BOTH, x_step),
            ring_of_4(q_w.reshape(-1, QC), "section", y_step),
        ),
    )
    q_w = q_w.reshape(D, QC)
    kv_w = kv_w.reshape(NX, NY, -1, KVC).transpose(1, 0, 2, 3).reshape(D, KVC)
    rest = rest.reshape(-1, AC + 2 * QC)

    x_oth = lax.ppermute(x_own, "ctx", CORE_SWAP)
    kv, q = project(0, lead, x_own, x_oth, kv_w, q_w, modulation, qk_gain)
    pending = {"rest": gather_x(after(rest, kv))}

    def fetch(k, event):
        rows = after(pending["rest"], event)
        if k == 1:
            pending["tail"] = gather_y(rows[:, :QC])
        if k == 2:
            pending["head"] = gather_y(after(rows[:, QC : QC + AC], pending["tail"]))

    att_own, att_oth = attention(kv, q, fetch)
    head_w = pending["head"]
    tail_w_own = after(pending["tail"], att_own)
    got_oth, got_own = (lax.ppermute(a, "ctx", CORE_SWAP) for a in (att_own, att_oth))
    tail_w_oth = lax.ppermute(tail_w_own, "ctx", CORE_SWAP)
    x_own, x_oth = output(
        0, lead, (att_own, got_own, att_oth, got_oth), (x_own, x_oth),
        tail_w_own, tail_w_oth, modulation,
    )

    kv, q = project(1, lead, x_own, x_oth, head_w[:, :KVC], head_w[:, KVC:], modulation, qk_gain)
    tail_new = lax.ppermute(after(x_own, kv), "section", section_step(-1))

    def swap_weights(k, event):
        if k == 0:
            pending["out"] = gather_y(after(pending["rest"][:, QC + AC :], event))
        if k == 2:
            pending["out"] = after(pending["out"], event)
            pending["swapped"] = lax.ppermute(pending["out"], "ctx", CORE_SWAP)

    att_own, att_oth = attention(kv, q, swap_weights)
    head_w_own, head_w_oth = pending["out"], pending["swapped"]
    got_own = lax.ppermute(att_oth, "ctx", CORE_SWAP)
    (head_new,) = output(
        1, lead, (att_own, got_own), (x_own,), head_w_own, head_w_oth, modulation
    )
    return (tail_new[None], head_new[None])


def solution(mesh):
    in_specs = (
        P("section", "ctx", None),
        P(),
        P(BOTH, None),
        P(BOTH, None),
        P(BOTH, None),
        P(BOTH, None),
        P(),
        P(),
    )
    out_specs = (P("section", "ctx", None), P("section", "ctx", None))
    return jax.shard_map(
        per_device, mesh=mesh, in_specs=in_specs, out_specs=out_specs, check_vma=False
    )
```

```python
import functools
import math

import jax
import jax.numpy as jnp
from jax import lax
from jax.experimental import pallas as pl
from jax.experimental.pallas import tpu as pltpu
from jax.sharding import PartitionSpec as P

D = 1536
HD = 128
GH = 3
QC = GH * HD
KVC = 2 * HD
AC = KVC + QC
TOK = 160
PAIR = 2 * TOK
NZ = 8
NX = 4
NY = 4
EPS = 1e-06
EXP2_SCALE = math.log2(math.e) * HD ** (-0.5)
VMEM = pl.BlockSpec(memory_space=pltpu.VMEM)
SMEM = pl.BlockSpec(memory_space=pltpu.SMEM)
BF = jnp.bfloat16
F32 = jnp.float32


def flat_id(x, y, z, c):
    return (y * 2 + (x >> 1)) * 32 + (x & 1) * 16 + z * 2 + c


CORE_SWAP = [(i, i ^ 1) for i in range(32)]
X_SWAP = [(i, i ^ 16) for i in range(32)]
ZC_GROUPS = [[xl * 16 + i for i in range(16)] for xl in range(2)]
XY_GROUPS = [
    [flat_id(x, y, z, c) for y in range(NY) for x in range(NX)] for z in range(NZ) for c in range(2)
]
BOTH = ("section", "ctx")


def z_step(by):
    return [(i, (i & 16) | ((((i >> 1) + by) % NZ) << 1) | (i & 1)) for i in range(32)]


def x_step(by):
    return [
        (flat_id(x, y, z, c), flat_id((x + by) % NX, y, z, c))
        for x in range(NX) for y in range(NY) for z in range(NZ) for c in range(2)
    ]


def y_step(by):
    return [(i, (((i >> 1) + by) % NY) << 1 | (i & 1)) for i in range(8)]


def section_step(by):
    return [(s, (s + by) % 8) for s in range(8)]


def cost(flops, nbytes, trans=0):
    return pl.CostEstimate(flops=int(flops), bytes_accessed=int(nbytes), transcendentals=int(trans))


def params():
    return pltpu.CompilerParams(vmem_limit_bytes=12 * 1024 * 1024)


def head_normal(values, gain_row):
    factor = lax.rsqrt(jnp.mean(values * values, axis=-1, keepdims=True) + EPS)
    return (values * factor * gain_row).astype(BF)


def project_body(layer, lead_ref, own_ref, oth_ref, wk_ref, wv_ref, wq_ref, mod_ref, gain_ref, kv_ref, q_ref, normed):
    row = mod_ref[layer, 0, pl.ds(lead_ref[0] + layer, 1), :]
    for part, ref in enumerate((own_ref, oth_ref)):
        x = ref[...].astype(F32)
        factor = lax.rsqrt(jnp.mean(x * x, axis=-1, keepdims=True) + EPS)
        normed[part * TOK : (part + 1) * TOK, :] = (x * factor * row).astype(BF)
    keys = jnp.dot(normed[...], wk_ref[...], preferred_element_type=F32)
    kv_ref[:, :HD] = head_normal(keys, gain_ref[layer, 1:2, :])
    vals = jnp.dot(normed[...], wv_ref[...], preferred_element_type=F32)
    kv_ref[:, HD:] = vals.astype(BF)
    for h in range(GH):
        q = jnp.dot(
            normed[...], wq_ref[:, h * HD : (h + 1) * HD], preferred_element_type=F32
        )
        q_ref[h] = head_normal(q, gain_ref[layer, 0:1, :])


def columns(array, width, block):
    return array, pl.BlockSpec((array.shape[0], width), lambda i: (0, block))


def whole(array):
    return array, pl.BlockSpec(array.shape, lambda i: (0,) * array.ndim)


def one_step(body, lead, operands, shapes, scratch, flops, name):
    arrays, specs = zip(*operands)
    return pl.pallas_call(
        body,
        grid=(1,),
        out_shape=shapes,
        in_specs=[SMEM, *specs],
        out_specs=tuple(
            pl.BlockSpec(s.shape, lambda i, n=len(s.shape): (0,) * n) for s in shapes
        ),
        scratch_shapes=scratch,
        compiler_params=params(),
        cost_estimate=cost(flops, 4 * 1024 * 1024),
        name=name,
    )(lead, *arrays)


def project(layer, lead, own, oth, w_keys, w_vals, w_queries, modulation, qk_gain):
    return one_step(
        functools.partial(project_body, layer),
        lead,
        (whole(own), whole(oth), w_keys, w_vals, w_queries, whole(modulation), whole(qk_gain)),
        (
            jax.ShapeDtypeStruct((PAIR, KVC), BF),
            jax.ShapeDtypeStruct((GH, PAIR, HD), BF),
        ),
        [pltpu.VMEM((PAIR, D), BF)],
        2 * PAIR * D * AC,
        "project",
    )


def add_keys(q, keys, vals):
    scores = lax.dot_general(q, keys, (((1,), (1,)), ((), ())), preferred_element_type=F32)
    weights = jnp.exp2(scores * EXP2_SCALE)
    return (
        jnp.dot(weights.astype(BF), vals, preferred_element_type=F32),
        jnp.sum(weights, axis=-1, keepdims=True),
    )


def attend_body(first, n_chunks, *refs):
    q_own, q_par = refs[:2]
    chunks = refs[2 : 2 + n_chunks]
    rest = refs[2 + n_chunks :]
    if first:
        num_out, den_out = rest
    else:
        num_in, den_in, num_out, den_out = rest
    def one_head(h, carry):
        for side, q_ref in enumerate((q_own, q_par)):
            q = q_ref[h]
            num = den = None
            for ref in chunks:
                part, total = add_keys(q, ref[:, :HD], ref[:, HD:])
                num = part if num is None else num + part
                den = total if den is None else den + total
            den = jnp.broadcast_to(den, (PAIR, HD))
            if not first:
                num = num + num_in[side * GH + h]
                den = den + den_in[side * GH + h]
            num_out[side * GH + h] = num
            den_out[side * GH + h] = den
        return carry

    lax.fori_loop(0, GH, one_head, 0)


def attend(q_own, q_par, chunks, state=None):
    shape = jax.ShapeDtypeStruct((2 * GH, PAIR, HD), F32)
    first = state is None
    n = len(chunks)
    return pl.pallas_call(
        functools.partial(attend_body, first, n),
        out_shape=(shape, shape),
        in_specs=[VMEM] * (2 + n + (0 if first else 2)),
        out_specs=(VMEM, VMEM),
        input_output_aliases={} if first else {2 + n: 0, 3 + n: 1},
        compiler_params=params(),
        cost_estimate=cost(
            2 * GH * PAIR * PAIR * n * HD * 4, 2 * 1024 * 1024, 2 * GH * PAIR * PAIR * n
        ),
        name="attend",
    )(q_own, q_par, *chunks, *(() if first else state))


def last_par_body(q_par, chunk, num_in, den_in, msg):
    keys, vals = chunk[:, :HD], chunk[:, HD:]
    lane = lax.broadcasted_iota(jnp.int32, (PAIR, HD), 1)
    plane = jnp.zeros((PAIR, HD), F32)
    for h in range(GH):
        num, den = add_keys(q_par[h], keys, vals)
        msg[h] = (num + num_in[GH + h]).astype(BF)
        den = jnp.broadcast_to(den, (PAIR, HD)) + den_in[GH + h]
        high = den.astype(BF).astype(F32)
        plane = jnp.where(lane == 2 * h, high, plane)
        plane = jnp.where(lane == 2 * h + 1, den - high, plane)
    msg[GH] = plane.astype(BF)


def last_own_body(q_own, chunk, num_in, den_in, num_out, den_out):
    keys, vals = chunk[:, :HD], chunk[:, HD:]
    for h in range(GH):
        num, den = add_keys(q_own[h], keys, vals)
        num_out[h] = num + num_in[h]
        den_out[h] = jnp.broadcast_to(den, (PAIR, HD)) + den_in[h]


def attend_last(q, chunk, state, own):
    shape = jax.ShapeDtypeStruct((GH, PAIR, HD), F32)
    message = jax.ShapeDtypeStruct((GH + 1, PAIR, HD), BF)
    return pl.pallas_call(
        last_own_body if own else last_par_body,
        out_shape=(shape, shape) if own else message,
        in_specs=[VMEM] * 4,
        out_specs=(VMEM, VMEM) if own else VMEM,
        compiler_params=params(),
        cost_estimate=cost(GH * PAIR * PAIR * HD * 4, 2 * 1024 * 1024, GH * PAIR * PAIR),
        name="attend_last",
    )(q, chunk, *state)


def merge_body(num_ref, den_ref, msg, out_own, out_oth):
    plane = msg[GH].astype(F32)
    for h in range(GH):
        den = den_ref[h][:, :1] + plane[:, 2 * h : 2 * h + 1] + plane[:, 2 * h + 1 : 2 * h + 2]
        value = ((num_ref[h] + msg[h].astype(F32)) / den).astype(BF)
        out_own[:, h * HD : (h + 1) * HD] = value[:TOK]
        out_oth[:, h * HD : (h + 1) * HD] = value[TOK:]


def merge(num, den, msg):
    shape = jax.ShapeDtypeStruct((TOK, QC), BF)
    return pl.pallas_call(
        merge_body,
        out_shape=(shape, shape),
        in_specs=[VMEM] * 3,
        out_specs=(VMEM, VMEM),
        compiler_params=params(),
        cost_estimate=cost(GH * PAIR * HD * 4, 1024 * 1024),
        name="merge",
    )(num, den, msg)


def output_body(layer, n, lead_ref, *refs):
    att, x, (w_own, w_oth, mod_ref), outs = (
        refs[: 2 * n],
        refs[2 * n : 3 * n],
        refs[3 * n : 3 * n + 3],
        refs[3 * n + 3 :],
    )
    gate = mod_ref[layer, 1, pl.ds(lead_ref[0] + layer, 1), :]
    dims = (((1,), (1,)), ((), ()))
    for part in range(n):
        update = lax.dot_general(att[2 * part][...], w_own[...], dims, preferred_element_type=F32)
        update += lax.dot_general(
            att[2 * part + 1][...], w_oth[...], dims, preferred_element_type=F32
        )
        outs[part][...] = (x[part][...].astype(F32) + gate * update).astype(BF)


def output(layer, lead, att, x, w_own, w_oth, modulation):
    n = len(x)
    return one_step(
        functools.partial(output_body, layer, n),
        lead,
        (*map(whole, att), *map(whole, x), w_own, w_oth, whole(modulation)),
        (jax.ShapeDtypeStruct((TOK, D), BF),) * n,
        [],
        2 * n * TOK * D * 2 * QC,
        "output",
    )


def after(value, *events):
    return lax.optimization_barrier((value, *events))[0]


def attention(kv, q, tick=lambda k, event: None):
    q_par = lax.ppermute(q, "ctx", X_SWAP)
    up = lax.ppermute(kv, "ctx", z_step(1))
    down = lax.ppermute(kv, "ctx", z_step(-1))
    tick(0, up)
    state = attend(q, q_par, (kv,))
    for k in range(2):
        next_up = lax.ppermute(up, "ctx", z_step(1))
        next_down = lax.ppermute(down, "ctx", z_step(-1))
        state = attend(q, q_par, (up, down), state)
        up, down, state = lax.optimization_barrier((next_up, next_down, state))
        tie = tick(k + 1, up)
        if tie is not None:
            up = after(up, tie)
    far = lax.ppermute(up, "ctx", z_step(1))
    state = attend(q, q_par, (up, down), state)
    msg = attend_last(q_par, far, state, False)
    got = lax.ppermute(msg, "ctx", X_SWAP)
    num, den = attend_last(q, far, after(state, msg), True)
    tick(3, num)
    return merge(num, den, got)


def assemble_body(tail_qkv, tail_out, head_qkv, head_out, near_ref, tq, to, hq, ho, sems):
    copies = [
        pltpu.make_async_copy(src, dst, sems.at[i])
        for i, (src, dst) in enumerate(
            ((tail_qkv, tq), (tail_out, to), (head_qkv, hq), (head_out, ho))
        )
    ]
    for copy in copies:
        copy.start()
    for copy in copies:
        copy.wait()
    nq, nk = 2 * QC, 2 * HD
    for c in range(2):

        def keys(ref):
            return ref[:, nq + c * HD : nq + (c + 1) * HD]

        def vals(ref):
            return ref[:, nq + nk + c * HD : nq + nk + (c + 1) * HD]

        def wide(ref):
            return ref[:, c * QC : (c + 1) * QC]

        row = jnp.concatenate(
            (keys(tq), vals(tq), wide(tq), wide(hq), wide(to), wide(ho), keys(hq), vals(hq)), axis=1
        )
        for z in range(NZ):
            near_ref[2 * z + c] = row


def assemble(tail_qkv, tail_out, head_qkv, head_out):
    args = [
        pltpu.with_memory_space_constraint(a, pltpu.MemorySpace.HBM)
        for a in (tail_qkv, tail_out, head_qkv, head_out)
    ]
    rows = tail_qkv.shape[0]
    return pl.pallas_call(
        assemble_body,
        out_shape=jax.ShapeDtypeStruct((2 * NZ, rows, 2 * AC + 2 * QC), BF),
        in_specs=[pl.BlockSpec(memory_space=pltpu.MemorySpace.HBM)] * 4,
        out_specs=VMEM,
        scratch_shapes=[pltpu.VMEM(a.shape, a.dtype) for a in args] + [pltpu.SemaphoreType.DMA((4,))],
        compiler_params=params(),
        cost_estimate=cost(0, 1024 * 1024),
        name="assemble",
    )(*args)


def place_body(n_sets, pos_ref, *refs):
    for k in range(n_sets):
        pieces, out = refs[4 * k : 4 * k + 4], refs[4 * n_sets + k]
        at = pos_ref[k]
        for ref, back in zip(pieces, (0, 1, 3, 2)):
            out[lax.rem(at + 4 - back, 4)] = ref[...]


def place(positions, sets):
    shapes = [jax.ShapeDtypeStruct((4, *pieces[0].shape), BF) for pieces in sets]
    return pl.pallas_call(
        functools.partial(place_body, len(sets)),
        out_shape=tuple(shapes),
        in_specs=[SMEM] + [VMEM] * (4 * len(sets)),
        out_specs=(VMEM,) * len(sets),
        compiler_params=params(),
        cost_estimate=cost(0, sum(8 * p[0].size for p in sets)),
        name="place",
    )(positions, *[p for pieces in sets for p in pieces])


def ring_of_4(rows, axis, step):
    return (rows, *(lax.ppermute(rows, axis, step(by)) for by in (1, -1, 2)))


def per_device(
    latent_state, lead_step, tail_qkv, tail_out, head_qkv, head_out, modulation, qk_gain
):
    section_pos = lax.axis_index("section")
    section_count = lax.axis_size("section")
    sender = jnp.mod(section_pos - 1 + section_count, section_count)
    lead = lax.dynamic_slice(lead_step, (sender,), (1,))
    x_own = lax.ppermute(latent_state[0], "section", section_step(1))

    near = assemble(tail_qkv, tail_out, head_qkv, head_out)
    near = lax.all_to_all(near, "ctx", 0, 0, axis_index_groups=ZC_GROUPS)
    near, x_own = lax.optimization_barrier((near, x_own))
    x_oth = lax.ppermute(x_own, "ctx", CORE_SWAP)
    near = near.reshape(-1, near.shape[-1])
    kv_w, q_w = near[:, :KVC], near[:, KVC:AC]
    later = lax.all_gather(
        near[:, AC:], BOTH, axis=0, tiled=True, axis_index_groups=XY_GROUPS
    )
    y_pos = section_pos // 2
    x_pos = (section_pos % 2) * 2 + lax.axis_index("ctx") // 16
    kv_w, q_w = place(
        jnp.stack([y_pos, x_pos]),
        (ring_of_4(kv_w, "section", y_step), ring_of_4(q_w, BOTH, x_step)),
    )
    kv_w, q_w, x_oth = lax.optimization_barrier((kv_w, q_w, x_oth))
    kv_w, q_w = place(
        jnp.stack([x_pos, y_pos]),
        (
            ring_of_4(kv_w.reshape(-1, KVC), BOTH, x_step),
            ring_of_4(q_w.reshape(-1, QC), "section", y_step),
        ),
    )
    q_w = q_w.reshape(D, QC)
    kv_w = kv_w.reshape(NX, NY, -1, KVC).transpose(1, 0, 2, 3).reshape(D, KVC)
    kv, q = project(
        0, lead, x_own, x_oth, columns(kv_w, HD, 0), columns(kv_w, HD, 1), whole(q_w), modulation, qk_gain
    )
    side = {}

    def beside_tail(k, event):
        if k == 3:
            side["later"] = after(later, event)
            side["out"] = lax.ppermute(side["later"][:, QC : 2 * QC], "ctx", CORE_SWAP)

    att_own, att_oth = attention(kv, q, beside_tail)
    got_oth, got_own = (lax.ppermute(a, "ctx", CORE_SWAP) for a in (att_own, att_oth))
    later, swapped = side["later"], side["out"]
    x_own, x_oth = output(
        0, lead, (att_own, got_own, att_oth, got_oth), (x_own, x_oth),
        columns(later, QC, 1), whole(swapped), modulation,
    )

    first_kv = 3 * QC // HD
    kv, q = project(
        1, lead, x_own, x_oth, columns(later, HD, first_kv), columns(later, HD, first_kv + 1),
        columns(later, QC, 0), modulation, qk_gain,
    )
    side["tail"] = lax.ppermute(x_own, "section", section_step(-1))

    def beside_head(k, event):
        if k == 1:
            return side["tail"]
        if k == 2:
            side["out"] = lax.ppermute(
                after(later[:, 2 * QC : 3 * QC], event), "ctx", CORE_SWAP
            )
        return None

    att_own, att_oth = attention(kv, q, beside_head)
    got_own = lax.ppermute(att_oth, "ctx", CORE_SWAP)
    (head_new,) = output(
        1, lead, (att_own, got_own), (x_own,), columns(later, QC, 2), whole(side["out"]), modulation
    )
    return (side["tail"][None], head_new[None])


def solution(mesh):
    in_specs = (
        P("section", "ctx", None),
        P(),
        P(BOTH, None),
        P(BOTH, None),
        P(BOTH, None),
        P(BOTH, None),
        P(),
        P(),
    )
    out_specs = (P("section", "ctx", None), P("section", "ctx", None))
    return jax.shard_map(
        per_device, mesh=mesh, in_specs=in_specs, out_specs=out_specs, check_vma=False
    )
```

```python
import functools
import math

import jax
import jax.numpy as jnp
from jax import lax
from jax.experimental import pallas as pl
from jax.experimental.pallas import tpu as pltpu
from jax.sharding import PartitionSpec as P

D = 1536
HD = 128
GH = 3
QC = GH * HD
KVC = 2 * HD
AC = KVC + QC
TOK = 160
PAIR = 2 * TOK
NZ = 8
NX = 4
NY = 4
EPS = 1e-06
EXP2_SCALE = math.log2(math.e) * HD ** (-0.5)
VMEM = pl.BlockSpec(memory_space=pltpu.VMEM)
SMEM = pl.BlockSpec(memory_space=pltpu.SMEM)
BF = jnp.bfloat16
F32 = jnp.float32


def flat_id(x, y, z, c):
    return (y * 2 + (x >> 1)) * 32 + (x & 1) * 16 + z * 2 + c


CORE_SWAP = [(i, i ^ 1) for i in range(32)]
X_SWAP = [(i, i ^ 16) for i in range(32)]
ZC_GROUPS = [[xl * 16 + i for i in range(16)] for xl in range(2)]
XY_GROUPS = [
    [flat_id(x, y, z, c) for y in range(NY) for x in range(NX)] for z in range(NZ) for c in range(2)
]
BOTH = ("section", "ctx")


def z_step(by):
    return [(i, (i & 16) | ((((i >> 1) + by) % NZ) << 1) | (i & 1)) for i in range(32)]


def x_step(by):
    return [
        (flat_id(x, y, z, c), flat_id((x + by) % NX, y, z, c))
        for x in range(NX) for y in range(NY) for z in range(NZ) for c in range(2)
    ]


def y_step(by):
    return [(i, (((i >> 1) + by) % NY) << 1 | (i & 1)) for i in range(8)]


def section_step(by):
    return [(s, (s + by) % 8) for s in range(8)]


def cost(flops, nbytes, trans=0):
    return pl.CostEstimate(flops=int(flops), bytes_accessed=int(nbytes), transcendentals=int(trans))


def params():
    return pltpu.CompilerParams(vmem_limit_bytes=12 * 1024 * 1024)


def head_normal(values, gain_row):
    factor = lax.rsqrt(jnp.mean(values * values, axis=-1, keepdims=True) + EPS)
    return (values * factor * gain_row).astype(BF)


def project_body(layer, lead_ref, own_ref, oth_ref, wk_ref, wv_ref, wq0_ref, wq1_ref, wq2_ref, mod_ref, gain_ref, kv_ref, q_ref, normed):
    row = mod_ref[layer, 0, pl.ds(lead_ref[0] + layer, 1), :]
    for part, ref in enumerate((own_ref, oth_ref)):
        x = ref[...].astype(F32)
        factor = lax.rsqrt(jnp.mean(x * x, axis=-1, keepdims=True) + EPS)
        normed[part * TOK : (part + 1) * TOK, :] = (x * factor * row).astype(BF)
    keys = jnp.dot(normed[...], wk_ref[...], preferred_element_type=F32)
    kv_ref[:, :HD] = head_normal(keys, gain_ref[layer, 1:2, :])
    vals = jnp.dot(normed[...], wv_ref[...], preferred_element_type=F32)
    kv_ref[:, HD:] = vals.astype(BF)
    for h, ref in enumerate((wq0_ref, wq1_ref, wq2_ref)):
        q = jnp.dot(normed[...], ref[...], preferred_element_type=F32)
        q_ref[h] = head_normal(q, gain_ref[layer, 0:1, :])


def columns(array, width, block):
    return array, pl.BlockSpec((array.shape[0], width), lambda i: (0, block))


def whole(array):
    return array, pl.BlockSpec(array.shape, lambda i: (0,) * array.ndim)


def one_step(body, lead, operands, shapes, scratch, flops, name):
    arrays, specs = zip(*operands)
    return pl.pallas_call(
        body,
        grid=(1,),
        out_shape=shapes,
        in_specs=[SMEM, *specs],
        out_specs=tuple(
            pl.BlockSpec(s.shape, lambda i, n=len(s.shape): (0,) * n) for s in shapes
        ),
        scratch_shapes=scratch,
        compiler_params=params(),
        cost_estimate=cost(flops, 4 * 1024 * 1024),
        name=name,
    )(lead, *arrays)


def project(layer, lead, own, oth, weights, modulation, qk_gain):
    return one_step(
        functools.partial(project_body, layer),
        lead,
        (whole(own), whole(oth), *weights, whole(modulation), whole(qk_gain)),
        (
            jax.ShapeDtypeStruct((PAIR, KVC), BF),
            jax.ShapeDtypeStruct((GH, PAIR, HD), BF),
        ),
        [pltpu.VMEM((PAIR, D), BF)],
        2 * PAIR * D * AC,
        "project",
    )


def add_keys(q, keys, vals):
    scores = lax.dot_general(q, keys, (((1,), (1,)), ((), ())), preferred_element_type=F32)
    weights = jnp.exp2(scores * EXP2_SCALE)
    return (
        jnp.dot(weights.astype(BF), vals, preferred_element_type=F32),
        jnp.sum(weights, axis=-1, keepdims=True),
    )


def attend_body(first, n_chunks, *refs):
    q_own, q_par = refs[:2]
    chunks = refs[2 : 2 + n_chunks]
    rest = refs[2 + n_chunks :]
    if first:
        num_out, den_out = rest
    else:
        num_in, den_in, num_out, den_out = rest
    def one_head(h, carry):
        for side, q_ref in enumerate((q_own, q_par)):
            q = q_ref[h]
            num = den = None
            for ref in chunks:
                part, total = add_keys(q, ref[:, :HD], ref[:, HD:])
                num = part if num is None else num + part
                den = total if den is None else den + total
            den = jnp.broadcast_to(den, (PAIR, HD))
            if not first:
                num = num + num_in[side * GH + h]
                den = den + den_in[side * GH + h]
            num_out[side * GH + h] = num
            den_out[side * GH + h] = den
        return carry

    lax.fori_loop(0, GH, one_head, 0)


def attend(q_own, q_par, chunks, state=None):
    shape = jax.ShapeDtypeStruct((2 * GH, PAIR, HD), F32)
    first = state is None
    n = len(chunks)
    return pl.pallas_call(
        functools.partial(attend_body, first, n),
        out_shape=(shape, shape),
        in_specs=[VMEM] * (2 + n + (0 if first else 2)),
        out_specs=(VMEM, VMEM),
        input_output_aliases={} if first else {2 + n: 0, 3 + n: 1},
        compiler_params=params(),
        cost_estimate=cost(
            2 * GH * PAIR * PAIR * n * HD * 4, 2 * 1024 * 1024, 2 * GH * PAIR * PAIR * n
        ),
        name="attend",
    )(q_own, q_par, *chunks, *(() if first else state))


def last_par_body(q_par, chunk, num_in, den_in, msg):
    keys, vals = chunk[:, :HD], chunk[:, HD:]
    lane = lax.broadcasted_iota(jnp.int32, (PAIR, HD), 1)
    plane = jnp.zeros((PAIR, HD), F32)
    for h in range(GH):
        num, den = add_keys(q_par[h], keys, vals)
        msg[h] = (num + num_in[GH + h]).astype(BF)
        den = jnp.broadcast_to(den, (PAIR, HD)) + den_in[GH + h]
        high = den.astype(BF).astype(F32)
        plane = jnp.where(lane == 2 * h, high, plane)
        plane = jnp.where(lane == 2 * h + 1, den - high, plane)
    msg[GH] = plane.astype(BF)


def last_own_body(q_own, chunk, num_in, den_in, num_out, den_out):
    keys, vals = chunk[:, :HD], chunk[:, HD:]
    for h in range(GH):
        num, den = add_keys(q_own[h], keys, vals)
        num_out[h] = num + num_in[h]
        den_out[h] = jnp.broadcast_to(den, (PAIR, HD)) + den_in[h]


def attend_last(q, chunk, state, own):
    shape = jax.ShapeDtypeStruct((GH, PAIR, HD), F32)
    message = jax.ShapeDtypeStruct((GH + 1, PAIR, HD), BF)
    return pl.pallas_call(
        last_own_body if own else last_par_body,
        out_shape=(shape, shape) if own else message,
        in_specs=[VMEM] * 4,
        out_specs=(VMEM, VMEM) if own else VMEM,
        compiler_params=params(),
        cost_estimate=cost(GH * PAIR * PAIR * HD * 4, 2 * 1024 * 1024, GH * PAIR * PAIR),
        name="attend_last",
    )(q, chunk, *state)


def merge_body(num_ref, den_ref, msg, out_own, out_oth):
    plane = msg[GH].astype(F32)
    for h in range(GH):
        den = den_ref[h][:, :1] + plane[:, 2 * h : 2 * h + 1] + plane[:, 2 * h + 1 : 2 * h + 2]
        value = ((num_ref[h] + msg[h].astype(F32)) / den).astype(BF)
        out_own[:, h * HD : (h + 1) * HD] = value[:TOK]
        out_oth[:, h * HD : (h + 1) * HD] = value[TOK:]


def merge(num, den, msg):
    shape = jax.ShapeDtypeStruct((TOK, QC), BF)
    return pl.pallas_call(
        merge_body,
        out_shape=(shape, shape),
        in_specs=[VMEM] * 3,
        out_specs=(VMEM, VMEM),
        compiler_params=params(),
        cost_estimate=cost(GH * PAIR * HD * 4, 1024 * 1024),
        name="merge",
    )(num, den, msg)


def output_body(layer, n, lead_ref, *refs):
    att, x, (w_own, w_oth, mod_ref), outs = (
        refs[: 2 * n],
        refs[2 * n : 3 * n],
        refs[3 * n : 3 * n + 3],
        refs[3 * n + 3 :],
    )
    gate = mod_ref[layer, 1, pl.ds(lead_ref[0] + layer, 1), :]
    dims = (((1,), (1,)), ((), ()))
    for part in range(n):
        update = lax.dot_general(att[2 * part][...], w_own[...], dims, preferred_element_type=F32)
        update += lax.dot_general(
            att[2 * part + 1][...], w_oth[...], dims, preferred_element_type=F32
        )
        outs[part][...] = (x[part][...].astype(F32) + gate * update).astype(BF)


def output(layer, lead, att, x, w_own, w_oth, modulation):
    n = len(x)
    return one_step(
        functools.partial(output_body, layer, n),
        lead,
        (*map(whole, att), *map(whole, x), w_own, w_oth, whole(modulation)),
        (jax.ShapeDtypeStruct((TOK, D), BF),) * n,
        [],
        2 * n * TOK * D * 2 * QC,
        "output",
    )


def after(value, *events):
    return lax.optimization_barrier((value, *events))[0]


def attention(kv, q, done_by_hop, tick):
    q_par = lax.ppermute(q, "ctx", X_SWAP)
    up = lax.ppermute(kv, "ctx", z_step(1))
    down = lax.ppermute(kv, "ctx", z_step(-1))
    waiting, state = [(kv,)], None
    for k, count in enumerate(done_by_hop):
        waiting.append((up, down))
        up = lax.ppermute(up, "ctx", z_step(1))
        down = lax.ppermute(down, "ctx", z_step(-1))
        for _ in range(count):
            state = attend(q, q_par, waiting.pop(0), state)
        if count:
            up, down, state = lax.optimization_barrier((up, down, state))
        tie = tick(k + 1, up)
        if tie is not None:
            up = after(up, tie)
    waiting.append((up, down))
    far = lax.ppermute(up, "ctx", z_step(1))
    for group in waiting:
        state = attend(q, q_par, group, state)
    msg = attend_last(q_par, far, state, False)
    got = lax.ppermute(msg, "ctx", X_SWAP)
    num, den = attend_last(q, far, after(state, msg), True)
    tick(3, num)
    return merge(num, den, got)


def assemble_body(tail_qkv, tail_out, head_qkv, head_out, near_ref, tq, to, hq, ho, sems):
    copies = [
        pltpu.make_async_copy(src, dst, sems.at[i])
        for i, (src, dst) in enumerate(
            ((tail_qkv, tq), (tail_out, to), (head_qkv, hq), (head_out, ho))
        )
    ]
    for copy in copies:
        copy.start()
    for copy in copies:
        copy.wait()
    nq, nk = 2 * QC, 2 * HD
    for c in range(2):

        def keys(ref):
            return ref[:, nq + c * HD : nq + (c + 1) * HD]

        def vals(ref):
            return ref[:, nq + nk + c * HD : nq + nk + (c + 1) * HD]

        def wide(ref):
            return ref[:, c * QC : (c + 1) * QC]

        row = jnp.concatenate(
            (keys(tq), vals(tq), wide(tq)[:, : 2 * HD], wide(to), wide(tq)[:, 2 * HD :],
             wide(hq), wide(ho), keys(hq), vals(hq)), axis=1
        )
        for z in range(NZ):
            near_ref[2 * z + c] = row


def assemble(tail_qkv, tail_out, head_qkv, head_out):
    args = [
        pltpu.with_memory_space_constraint(a, pltpu.MemorySpace.HBM)
        for a in (tail_qkv, tail_out, head_qkv, head_out)
    ]
    rows = tail_qkv.shape[0]
    return pl.pallas_call(
        assemble_body,
        out_shape=jax.ShapeDtypeStruct((2 * NZ, rows, 2 * AC + 2 * QC), BF),
        in_specs=[pl.BlockSpec(memory_space=pltpu.MemorySpace.HBM)] * 4,
        out_specs=VMEM,
        scratch_shapes=[pltpu.VMEM(a.shape, a.dtype) for a in args] + [pltpu.SemaphoreType.DMA((4,))],
        compiler_params=params(),
        cost_estimate=cost(0, 1024 * 1024),
        name="assemble",
    )(*args)


def place_body(n_sets, pos_ref, *refs):
    for k in range(n_sets):
        pieces, out = refs[4 * k : 4 * k + 4], refs[4 * n_sets + k]
        at = pos_ref[k]
        for ref, back in zip(pieces, (0, 1, 3, 2)):
            out[lax.rem(at + 4 - back, 4)] = ref[...]


def place(positions, sets):
    shapes = [jax.ShapeDtypeStruct((4, *pieces[0].shape), BF) for pieces in sets]
    return pl.pallas_call(
        functools.partial(place_body, len(sets)),
        out_shape=tuple(shapes),
        in_specs=[SMEM] + [VMEM] * (4 * len(sets)),
        out_specs=(VMEM,) * len(sets),
        compiler_params=params(),
        cost_estimate=cost(0, sum(8 * p[0].size for p in sets)),
        name="place",
    )(positions, *[p for pieces in sets for p in pieces])


def ring_of_4(rows, axis, step):
    return (rows, *(lax.ppermute(rows, axis, step(by)) for by in (1, -1, 2)))


def per_device(
    latent_state, lead_step, tail_qkv, tail_out, head_qkv, head_out, modulation, qk_gain
):
    section_pos = lax.axis_index("section")
    section_count = lax.axis_size("section")
    sender = jnp.mod(section_pos - 1 + section_count, section_count)
    lead = lax.dynamic_slice(lead_step, (sender,), (1,))
    x_own = lax.ppermute(latent_state[0], "section", section_step(1))

    near = assemble(tail_qkv, tail_out, head_qkv, head_out)
    near = lax.all_to_all(near, "ctx", 0, 0, axis_index_groups=ZC_GROUPS)
    near, x_own = lax.optimization_barrier((near, x_own))
    x_oth = lax.ppermute(x_own, "ctx", CORE_SWAP)
    near = near.reshape(-1, near.shape[-1])
    half = KVC + 2 * HD
    by_x, by_y = near[:, :half], near[:, half : 2 * half]
    later = lax.all_gather(
        near[:, 2 * half :], BOTH, axis=0, tiled=True, axis_index_groups=XY_GROUPS
    )
    y_pos = section_pos // 2
    x_pos = (section_pos % 2) * 2 + lax.axis_index("ctx") // 16
    by_y, by_x = place(
        jnp.stack([y_pos, x_pos]),
        (ring_of_4(by_y, "section", y_step), ring_of_4(by_x, BOTH, x_step)),
    )
    by_y, by_x, x_oth = lax.optimization_barrier((by_y, by_x, x_oth))
    by_y, by_x = place(
        jnp.stack([x_pos, y_pos]),
        (
            ring_of_4(by_y.reshape(-1, half), BOTH, x_step),
            ring_of_4(by_x.reshape(-1, half), "section", y_step),
        ),
    )
    by_x = by_x.reshape(D, half)
    by_y = by_y.reshape(NX, NY, -1, half).transpose(1, 0, 2, 3).reshape(D, half)
    kv, q = project(
        0, lead, x_own, x_oth, [columns(by_x, HD, i) for i in range(4)] + [columns(by_y, HD, 3)],
        modulation, qk_gain,
    )
    side = {}

    def beside_tail(k, event):
        if k == 1:
            side["out"] = lax.ppermute(after(by_y, event), "ctx", CORE_SWAP)

    att_own, att_oth = attention(kv, q, (2, 1), beside_tail)
    got_oth, got_own = (lax.ppermute(a, "ctx", CORE_SWAP) for a in (att_own, att_oth))
    x_own, x_oth = output(
        0, lead, (att_own, got_own, att_oth, got_oth), (x_own, x_oth),
        columns(by_y, QC, 0), columns(side["out"], QC, 0), modulation,
    )

    kv, q = project(
        1, lead, x_own, x_oth, [columns(later, HD, i) for i in (6, 7, 0, 1, 2)], modulation, qk_gain
    )
    side["tail"] = lax.ppermute(after(x_own, q), "section", section_step(-1))

    def beside_head(k, event):
        if k == 1:
            return side["tail"]
        if k == 2:
            side["out"] = lax.ppermute(
                after(later[:, QC : 2 * QC], event), "ctx", CORE_SWAP
            )
        return None

    att_own, att_oth = attention(kv, q, (0, 2), beside_head)
    got_own = lax.ppermute(att_oth, "ctx", CORE_SWAP)
    (head_new,) = output(
        1, lead, (att_own, got_own), (x_own,), columns(later, QC, 1), whole(side["out"]), modulation
    )
    return (side["tail"][None], head_new[None])


def solution(mesh):
    in_specs = (
        P("section", "ctx", None),
        P(),
        P(BOTH, None),
        P(BOTH, None),
        P(BOTH, None),
        P(BOTH, None),
        P(),
        P(),
    )
    out_specs = (P("section", "ctx", None), P("section", "ctx", None))
    return jax.shard_map(
        per_device, mesh=mesh, in_specs=in_specs, out_specs=out_specs, check_vma=False
    )
```

```python
import functools
import math

import jax
import jax.numpy as jnp
from jax import lax
from jax.experimental import pallas as pl
from jax.experimental.pallas import tpu as pltpu
from jax.sharding import PartitionSpec as P

D = 1536
HD = 128
GH = 3
QC = GH * HD
KVC = 2 * HD
AC = KVC + QC
TOK = 160
PAIR = 2 * TOK
NZ = 8
NX = 4
NY = 4
EPS = 1e-06
EXP2_SCALE = math.log2(math.e) * HD ** (-0.5)
VMEM = pl.BlockSpec(memory_space=pltpu.VMEM)
SMEM = pl.BlockSpec(memory_space=pltpu.SMEM)
BF = jnp.bfloat16
F32 = jnp.float32


def flat_id(x, y, z, c):
    return (y * 2 + (x >> 1)) * 32 + (x & 1) * 16 + z * 2 + c


CORE_SWAP = [(i, i ^ 1) for i in range(32)]
X_SWAP = [(i, i ^ 16) for i in range(32)]
ZC_GROUPS = [[xl * 16 + i for i in range(16)] for xl in range(2)]
XY_GROUPS = [
    [flat_id(x, y, z, c) for y in range(NY) for x in range(NX)] for z in range(NZ) for c in range(2)
]
BOTH = ("section", "ctx")


def z_step(by):
    return [(i, (i & 16) | ((((i >> 1) + by) % NZ) << 1) | (i & 1)) for i in range(32)]


def x_step(by):
    return [
        (flat_id(x, y, z, c), flat_id((x + by) % NX, y, z, c))
        for x in range(NX) for y in range(NY) for z in range(NZ) for c in range(2)
    ]


def y_step(by):
    return [(i, (((i >> 1) + by) % NY) << 1 | (i & 1)) for i in range(8)]


def section_step(by):
    return [(s, (s + by) % 8) for s in range(8)]


def cost(flops, nbytes, trans=0):
    return pl.CostEstimate(flops=int(flops), bytes_accessed=int(nbytes), transcendentals=int(trans))


def params():
    return pltpu.CompilerParams(vmem_limit_bytes=12 * 1024 * 1024)


def sample_lead(lead_ref):
    return lead_ref[lax.rem(lax.axis_index("section") + 7, 8)]


def head_normal(values, gain_row):
    factor = lax.rsqrt(jnp.mean(values * values, axis=-1, keepdims=True) + EPS)
    return (values * factor * gain_row).astype(BF)


def project_kv_body(layer, lead_ref, own_ref, oth_ref, wk_ref, wv_ref, mod_ref, gain_ref, kv_ref, normed):
    row = mod_ref[layer, 0, pl.ds(sample_lead(lead_ref) + layer, 1), :]
    for part, ref in enumerate((own_ref, oth_ref)):
        x = ref[...].astype(F32)
        factor = lax.rsqrt(jnp.mean(x * x, axis=-1, keepdims=True) + EPS)
        normed[part * TOK : (part + 1) * TOK, :] = (x * factor * row).astype(BF)
    keys = jnp.dot(normed[...], wk_ref[...], preferred_element_type=F32)
    kv_ref[:, :HD] = head_normal(keys, gain_ref[layer, 1:2, :])
    vals = jnp.dot(normed[...], wv_ref[...], preferred_element_type=F32)
    kv_ref[:, HD:] = vals.astype(BF)


def project_q_body(layer, normed, wq_ref, gain_ref, q_ref):
    for h in range(GH):
        q = jnp.dot(
            normed[...], wq_ref[:, h * HD : (h + 1) * HD], preferred_element_type=F32
        )
        q_ref[h] = head_normal(q, gain_ref[layer, 0:1, :])


def columns(array, width, block):
    return array, pl.BlockSpec((array.shape[0], width), lambda i: (0, block))


def whole(array):
    return array, pl.BlockSpec(array.shape, lambda i: (0,) * array.ndim)


def one_step(body, lead, operands, shapes, flops, name):
    arrays, specs = zip(*operands)
    if lead is not None:
        arrays, specs = (lead, *arrays), (SMEM, *specs)
    return pl.pallas_call(
        body,
        grid=(1,),
        out_shape=shapes,
        in_specs=list(specs),
        out_specs=tuple(
            pl.BlockSpec(s.shape, lambda i, n=len(s.shape): (0,) * n) for s in shapes
        ),
        compiler_params=params(),
        cost_estimate=cost(flops, 4 * 1024 * 1024),
        name=name,
    )(*arrays)


def project_kv(layer, lead, own, oth, w_keys, w_vals, modulation, qk_gain):
    return one_step(
        functools.partial(project_kv_body, layer),
        lead,
        (whole(own), whole(oth), w_keys, w_vals, whole(modulation), whole(qk_gain)),
        (jax.ShapeDtypeStruct((PAIR, KVC), BF), jax.ShapeDtypeStruct((PAIR, D), BF)),
        2 * PAIR * D * KVC,
        "project_kv",
    )


def project_q(layer, normed, w_queries, qk_gain):
    (q,) = one_step(
        functools.partial(project_q_body, layer),
        None,
        (whole(normed), w_queries, whole(qk_gain)),
        (jax.ShapeDtypeStruct((GH, PAIR, HD), BF),),
        2 * PAIR * D * QC,
        "project_q",
    )
    return q


def add_keys(q, keys, vals):
    scores = lax.dot_general(q, keys, (((1,), (1,)), ((), ())), preferred_element_type=F32)
    weights = jnp.exp2(scores * EXP2_SCALE)
    return (
        jnp.dot(weights.astype(BF), vals, preferred_element_type=F32),
        jnp.sum(weights, axis=-1, keepdims=True),
    )


def attend_body(first, n_chunks, *refs):
    q_own, q_par = refs[:2]
    chunks = refs[2 : 2 + n_chunks]
    rest = refs[2 + n_chunks :]
    if first:
        num_out, den_out = rest
    else:
        num_in, den_in, num_out, den_out = rest
    def one_head(h, carry):
        for side, q_ref in enumerate((q_own, q_par)):
            q = q_ref[h]
            num = den = None
            for ref in chunks:
                part, total = add_keys(q, ref[:, :HD], ref[:, HD:])
                num = part if num is None else num + part
                den = total if den is None else den + total
            den = jnp.broadcast_to(den, (PAIR, HD))
            if not first:
                num = num + num_in[side * GH + h]
                den = den + den_in[side * GH + h]
            num_out[side * GH + h] = num
            den_out[side * GH + h] = den
        return carry

    lax.fori_loop(0, GH, one_head, 0)


def attend(q_own, q_par, chunks, state=None):
    shape = jax.ShapeDtypeStruct((2 * GH, PAIR, HD), F32)
    first = state is None
    n = len(chunks)
    return pl.pallas_call(
        functools.partial(attend_body, first, n),
        out_shape=(shape, shape),
        in_specs=[VMEM] * (2 + n + (0 if first else 2)),
        out_specs=(VMEM, VMEM),
        input_output_aliases={} if first else {2 + n: 0, 3 + n: 1},
        compiler_params=params(),
        cost_estimate=cost(
            2 * GH * PAIR * PAIR * n * HD * 4, 2 * 1024 * 1024, 2 * GH * PAIR * PAIR * n
        ),
        name="attend",
    )(q_own, q_par, *chunks, *(() if first else state))


def last_par_body(q_par, chunk, num_in, den_in, msg):
    keys, vals = chunk[:, :HD], chunk[:, HD:]
    lane = lax.broadcasted_iota(jnp.int32, (PAIR, HD), 1)
    plane = jnp.zeros((PAIR, HD), F32)
    for h in range(GH):
        num, den = add_keys(q_par[h], keys, vals)
        msg[h] = (num + num_in[GH + h]).astype(BF)
        den = jnp.broadcast_to(den, (PAIR, HD)) + den_in[GH + h]
        high = den.astype(BF).astype(F32)
        plane = jnp.where(lane == 2 * h, high, plane)
        plane = jnp.where(lane == 2 * h + 1, den - high, plane)
    msg[GH] = plane.astype(BF)


def last_own_body(q_own, chunk, num_in, den_in, num_out, den_out):
    keys, vals = chunk[:, :HD], chunk[:, HD:]
    for h in range(GH):
        num, den = add_keys(q_own[h], keys, vals)
        num_out[h] = num + num_in[h]
        den_out[h] = jnp.broadcast_to(den, (PAIR, HD)) + den_in[h]


def attend_last(q, chunk, state, own):
    shape = jax.ShapeDtypeStruct((GH, PAIR, HD), F32)
    message = jax.ShapeDtypeStruct((GH + 1, PAIR, HD), BF)
    return pl.pallas_call(
        last_own_body if own else last_par_body,
        out_shape=(shape, shape) if own else message,
        in_specs=[VMEM] * 4,
        out_specs=(VMEM, VMEM) if own else VMEM,
        compiler_params=params(),
        cost_estimate=cost(GH * PAIR * PAIR * HD * 4, 2 * 1024 * 1024, GH * PAIR * PAIR),
        name="attend_last",
    )(q, chunk, *state)


def merge_body(num_ref, den_ref, msg, out_own, out_oth):
    plane = msg[GH].astype(F32)
    for h in range(GH):
        den = den_ref[h][:, :1] + plane[:, 2 * h : 2 * h + 1] + plane[:, 2 * h + 1 : 2 * h + 2]
        value = ((num_ref[h] + msg[h].astype(F32)) / den).astype(BF)
        out_own[:, h * HD : (h + 1) * HD] = value[:TOK]
        out_oth[:, h * HD : (h + 1) * HD] = value[TOK:]


def merge(num, den, msg):
    shape = jax.ShapeDtypeStruct((TOK, QC), BF)
    return pl.pallas_call(
        merge_body,
        out_shape=(shape, shape),
        in_specs=[VMEM] * 3,
        out_specs=(VMEM, VMEM),
        compiler_params=params(),
        cost_estimate=cost(GH * PAIR * HD * 4, 1024 * 1024),
        name="merge",
    )(num, den, msg)


def output_body(layer, n, lead_ref, *refs):
    att, x, (w_own, w_oth, mod_ref), outs = (
        refs[: 2 * n],
        refs[2 * n : 3 * n],
        refs[3 * n : 3 * n + 3],
        refs[3 * n + 3 :],
    )
    gate = mod_ref[layer, 1, pl.ds(sample_lead(lead_ref) + layer, 1), :]
    dims = (((1,), (1,)), ((), ()))
    for part in range(n):
        update = lax.dot_general(att[2 * part][...], w_own[...], dims, preferred_element_type=F32)
        update += lax.dot_general(
            att[2 * part + 1][...], w_oth[...], dims, preferred_element_type=F32
        )
        outs[part][...] = (x[part][...].astype(F32) + gate * update).astype(BF)


def output(layer, lead, att, x, w_own, w_oth, modulation):
    n = len(x)
    return one_step(
        functools.partial(output_body, layer, n),
        lead,
        (*map(whole, att), *map(whole, x), w_own, w_oth, whole(modulation)),
        (jax.ShapeDtypeStruct((TOK, D), BF),) * n,
        2 * n * TOK * D * 2 * QC,
        "output",
    )


def after(value, *events):
    return lax.optimization_barrier((value, *events))[0]


def attention(kv, make_q, q_first, done_by_hop, tick):
    up = lax.ppermute(kv, "ctx", z_step(1))
    down = lax.ppermute(kv, "ctx", z_step(-1))
    waiting, state = [(kv,), (up, down)], None
    next_up = lax.ppermute(up, "ctx", z_step(1))
    next_down = lax.ppermute(down, "ctx", z_step(-1))
    if not q_first:
        next_up, next_down = lax.optimization_barrier((next_up, next_down))
    q = make_q(next_up)
    q_par = lax.ppermute(q, "ctx", X_SWAP)
    tick(0, q_par)
    for k, count in enumerate(done_by_hop):
        if k:
            waiting.append((up, down))
            next_up = lax.ppermute(up, "ctx", z_step(1))
            next_down = lax.ppermute(down, "ctx", z_step(-1))
        up, down = next_up, next_down
        for _ in range(count):
            state = attend(q, q_par, waiting.pop(0), state)
        if count:
            up, down, state = lax.optimization_barrier((up, down, state))
        tie = tick(k + 1, up)
        if tie is not None:
            up = after(up, *tie)
    waiting.append((up, down))
    far = lax.ppermute(up, "ctx", z_step(1))
    for group in waiting:
        state = attend(q, q_par, group, state)
    msg = attend_last(q_par, far, state, False)
    got = lax.ppermute(msg, "ctx", X_SWAP)
    num, den = attend_last(q, far, after(state, msg), True)
    tick(3, num)
    return merge(num, den, got)


def assemble_body(tail_qkv, tail_out, head_qkv, head_out, near_ref, tq, to, hq, ho, sems):
    copies = [
        pltpu.make_async_copy(src, dst, sems.at[i])
        for i, (src, dst) in enumerate(
            ((tail_qkv, tq), (tail_out, to), (head_qkv, hq), (head_out, ho))
        )
    ]
    for copy in copies:
        copy.start()
    for copy in copies:
        copy.wait()
    nq, nk = 2 * QC, 2 * HD
    for c in range(2):

        def keys(ref):
            return ref[:, nq + c * HD : nq + (c + 1) * HD]

        def vals(ref):
            return ref[:, nq + nk + c * HD : nq + nk + (c + 1) * HD]

        def wide(ref):
            return ref[:, c * QC : (c + 1) * QC]

        row = jnp.concatenate(
            (keys(tq), vals(tq), wide(tq), wide(to), wide(hq), wide(ho), keys(hq), vals(hq)), axis=1
        )
        for z in range(NZ):
            near_ref[2 * z + c] = row


def assemble(tail_qkv, tail_out, head_qkv, head_out):
    args = [
        pltpu.with_memory_space_constraint(a, pltpu.MemorySpace.HBM)
        for a in (tail_qkv, tail_out, head_qkv, head_out)
    ]
    rows = tail_qkv.shape[0]
    return pl.pallas_call(
        assemble_body,
        out_shape=jax.ShapeDtypeStruct((2 * NZ, rows, 2 * AC + 2 * QC), BF),
        in_specs=[pl.BlockSpec(memory_space=pltpu.MemorySpace.HBM)] * 4,
        out_specs=VMEM,
        scratch_shapes=[pltpu.VMEM(a.shape, a.dtype) for a in args] + [pltpu.SemaphoreType.DMA((4,))],
        compiler_params=params(),
        cost_estimate=cost(0, 1024 * 1024),
        name="assemble",
    )(*args)


def position(axis):
    if axis == "y":
        return lax.axis_index("section") // 2
    return lax.rem(lax.axis_index("section"), 2) * 2 + lax.axis_index("ctx") // 16


def place_body(axes, n_outs, *refs):
    outs = refs[4 * len(axes) :]
    for k, axis in enumerate(axes):
        at = position(axis)
        mine, outs = outs[: n_outs[k]], outs[n_outs[k] :]
        for ref, back in zip(refs[4 * k : 4 * k + 4], (0, 1, 3, 2)):
            start = 0
            for out in mine:
                width = out.shape[-1]
                out[lax.rem(at + 4 - back, 4)] = ref[:, start : start + width]
                start += width


def place(axes, sets, widths):
    shapes = [
        jax.ShapeDtypeStruct((4, pieces[0].shape[0], width), BF)
        for pieces, parts in zip(sets, widths)
        for width in parts
    ]
    return pl.pallas_call(
        functools.partial(place_body, axes, [len(parts) for parts in widths]),
        out_shape=tuple(shapes),
        in_specs=[VMEM] * (4 * len(sets)),
        out_specs=(VMEM,) * len(shapes),
        compiler_params=params(),
        cost_estimate=cost(0, sum(8 * p[0].size for p in sets)),
        name="place",
    )(*[p for pieces in sets for p in pieces])


def ring_of_4(rows, axis, step):
    return (rows, *(lax.ppermute(rows, axis, step(by)) for by in (1, -1, 2)))


def per_device(
    latent_state, lead_step, tail_qkv, tail_out, head_qkv, head_out, modulation, qk_gain
):
    x_own = lax.ppermute(latent_state[0], "section", section_step(1))

    near = assemble(tail_qkv, tail_out, head_qkv, head_out)
    near = lax.all_to_all(near, "ctx", 0, 0, axis_index_groups=ZC_GROUPS)
    near, x_own = lax.optimization_barrier((near, x_own))
    x_oth = lax.ppermute(x_own, "ctx", CORE_SWAP)
    near = near.reshape(-1, near.shape[-1])
    kv_w, wide_w = near[:, :KVC], after(near[:, KVC : AC + QC], x_oth)
    later = lax.all_gather(
        near[:, AC + QC :], BOTH, axis=0, tiled=True, axis_index_groups=XY_GROUPS
    )
    (kv_w,) = place("y", (ring_of_4(kv_w, "section", y_step),), ((KVC,),))
    kv_w, x_oth = lax.optimization_barrier((kv_w, x_oth))
    (wide_w,) = place("x", (ring_of_4(wide_w, BOTH, x_step),), ((2 * QC,),))
    kv_first = kv_w
    (kv_w,) = place("x", (ring_of_4(kv_w.reshape(-1, KVC), BOTH, x_step),), ((KVC,),))
    q_w, out_w = place(
        "y", (ring_of_4(after(wide_w.reshape(-1, 2 * QC), kv_first), "section", y_step),), ((QC, QC),)
    )
    q_w, out_w = q_w.reshape(D, QC), out_w.reshape(D, QC)
    kv_w = kv_w.reshape(NX, NY, -1, KVC).transpose(1, 0, 2, 3).reshape(D, KVC)
    kv, normed = project_kv(
        0, lead_step, x_own, x_oth, columns(kv_w, HD, 0), columns(kv_w, HD, 1), modulation, qk_gain
    )
    side = {}

    def beside_tail(k, event):
        if k == 0:
            side["out"] = lax.ppermute(after(out_w, event), "ctx", CORE_SWAP)

    att_own, att_oth = attention(
        kv, lambda event: project_q(0, after(normed, event), whole(q_w), qk_gain), False, (0, 1), beside_tail
    )
    got_oth, got_own = (lax.ppermute(a, "ctx", CORE_SWAP) for a in (att_own, att_oth))
    x_own, x_oth = output(
        0, lead_step, (att_own, got_own, att_oth, got_oth), (x_own, x_oth),
        whole(out_w), whole(side["out"]), modulation,
    )

    kv, normed = project_kv(
        1, lead_step, x_own, x_oth, columns(later, HD, 6), columns(later, HD, 7), modulation, qk_gain
    )
    q = project_q(1, normed, columns(later, QC, 0), qk_gain)
    side["tail"] = lax.ppermute(after(x_own, q), "section", section_step(-1))

    def beside_head(k, event):
        if k == 1:
            return (side["tail"],)
        if k == 2:
            side["out"] = lax.ppermute(
                after(later[:, QC : 2 * QC], event), "ctx", CORE_SWAP
            )
        return None

    att_own, att_oth = attention(kv, lambda event: q, True, (0, 2), beside_head)
    got_own = lax.ppermute(att_oth, "ctx", CORE_SWAP)
    (head_new,) = output(
        1, lead_step, (att_own, got_own), (x_own,), columns(later, QC, 1), whole(side["out"]), modulation
    )
    return (side["tail"][None], head_new[None])


def solution(mesh):
    in_specs = (
        P("section", "ctx", None),
        P(),
        P(BOTH, None),
        P(BOTH, None),
        P(BOTH, None),
        P(BOTH, None),
        P(),
        P(),
    )
    out_specs = (P("section", "ctx", None), P("section", "ctx", None))
    return jax.shard_map(
        per_device, mesh=mesh, in_specs=in_specs, out_specs=out_specs, check_vma=False
    )
```

```python
import functools
import math

import jax
import jax.numpy as jnp
from jax import lax
from jax.experimental import pallas as pl
from jax.experimental.pallas import tpu as pltpu
from jax.sharding import PartitionSpec as P

D = 1536
HD = 128
GH = 3
QC = GH * HD
KVC = 2 * HD
AC = KVC + QC
TOK = 160
PAIR = 2 * TOK
NZ = 8
NX = 4
NY = 4
EPS = 1e-06
EXP2_SCALE = math.log2(math.e) * HD ** (-0.5)
VMEM = pl.BlockSpec(memory_space=pltpu.VMEM)
SMEM = pl.BlockSpec(memory_space=pltpu.SMEM)
BF = jnp.bfloat16
F32 = jnp.float32


def flat_id(x, y, z, c):
    return (y * 2 + (x >> 1)) * 32 + (x & 1) * 16 + z * 2 + c


CORE_SWAP = [(i, i ^ 1) for i in range(32)]
X_SWAP = [(i, i ^ 16) for i in range(32)]
ZC_GROUPS = [[xl * 16 + i for i in range(16)] for xl in range(2)]
XY_GROUPS = [
    [flat_id(x, y, z, c) for y in range(NY) for x in range(NX)] for z in range(NZ) for c in range(2)
]
BOTH = ("section", "ctx")


def z_step(by):
    return [(i, (i & 16) | ((((i >> 1) + by) % NZ) << 1) | (i & 1)) for i in range(32)]


def x_step(by):
    return [
        (flat_id(x, y, z, c), flat_id((x + by) % NX, y, z, c))
        for x in range(NX) for y in range(NY) for z in range(NZ) for c in range(2)
    ]


def y_step(by):
    return [(i, (((i >> 1) + by) % NY) << 1 | (i & 1)) for i in range(8)]


def section_step(by):
    return [(s, (s + by) % 8) for s in range(8)]


def cost(flops, nbytes, trans=0):
    return pl.CostEstimate(flops=int(flops), bytes_accessed=int(nbytes), transcendentals=int(trans))


def params():
    return pltpu.CompilerParams(vmem_limit_bytes=12 * 1024 * 1024)


def sample_lead(lead_ref):
    return lead_ref[lax.rem(lax.axis_index("section") + 7, 8)]


def head_normal(values, gain_row):
    factor = lax.rsqrt(jnp.mean(values * values, axis=-1, keepdims=True) + EPS)
    return (values * factor * gain_row).astype(BF)


def project_body(layer, lead_ref, own_ref, oth_ref, wk_ref, wv_ref, wq0_ref, wq1_ref, wq2_ref, mod_ref, gain_ref, kv_ref, q_ref, normed):
    row = mod_ref[layer, 0, pl.ds(sample_lead(lead_ref) + layer, 1), :]
    for part, ref in enumerate((own_ref, oth_ref)):
        x = ref[...].astype(F32)
        factor = lax.rsqrt(jnp.mean(x * x, axis=-1, keepdims=True) + EPS)
        normed[part * TOK : (part + 1) * TOK, :] = (x * factor * row).astype(BF)
    keys = jnp.dot(normed[...], wk_ref[...], preferred_element_type=F32)
    kv_ref[:, :HD] = head_normal(keys, gain_ref[layer, 1:2, :])
    vals = jnp.dot(normed[...], wv_ref[...], preferred_element_type=F32)
    kv_ref[:, HD:] = vals.astype(BF)
    for h, ref in enumerate((wq0_ref, wq1_ref, wq2_ref)):
        q = jnp.dot(normed[...], ref[...], preferred_element_type=F32)
        q_ref[h] = head_normal(q, gain_ref[layer, 0:1, :])


def columns(array, width, block):
    return array, pl.BlockSpec((array.shape[0], width), lambda i: (0, block))


def whole(array):
    return array, pl.BlockSpec(array.shape, lambda i: (0,) * array.ndim)


def one_step(body, lead, operands, shapes, scratch, flops, name):
    arrays, specs = zip(*operands)
    return pl.pallas_call(
        body,
        grid=(1,),
        out_shape=shapes,
        in_specs=[SMEM, *specs],
        out_specs=tuple(
            pl.BlockSpec(s.shape, lambda i, n=len(s.shape): (0,) * n) for s in shapes
        ),
        scratch_shapes=scratch,
        compiler_params=params(),
        cost_estimate=cost(flops, 4 * 1024 * 1024),
        name=name,
    )(lead, *arrays)


def project(layer, lead, own, oth, weights, modulation, qk_gain):
    return one_step(
        functools.partial(project_body, layer),
        lead,
        (whole(own), whole(oth), *weights, whole(modulation), whole(qk_gain)),
        (
            jax.ShapeDtypeStruct((PAIR, KVC), BF),
            jax.ShapeDtypeStruct((GH, PAIR, HD), BF),
        ),
        [pltpu.VMEM((PAIR, D), BF)],
        2 * PAIR * D * AC,
        "project",
    )


def add_keys(q, keys, vals):
    scores = lax.dot_general(q, keys, (((1,), (1,)), ((), ())), preferred_element_type=F32)
    weights = jnp.exp2(scores * EXP2_SCALE)
    return (
        jnp.dot(weights.astype(BF), vals, preferred_element_type=F32),
        jnp.sum(weights, axis=-1, keepdims=True),
    )


def attend_body(first, n_chunks, *refs):
    q_own, q_par = refs[:2]
    chunks = refs[2 : 2 + n_chunks]
    rest = refs[2 + n_chunks :]
    if first:
        num_out, den_out = rest
    else:
        num_in, den_in, num_out, den_out = rest
    def one_head(h, carry):
        for side, q_ref in enumerate((q_own, q_par)):
            q = q_ref[h]
            num = den = None
            for ref in chunks:
                part, total = add_keys(q, ref[:, :HD], ref[:, HD:])
                num = part if num is None else num + part
                den = total if den is None else den + total
            den = jnp.broadcast_to(den, (PAIR, HD))
            if not first:
                num = num + num_in[side * GH + h]
                den = den + den_in[side * GH + h]
            num_out[side * GH + h] = num
            den_out[side * GH + h] = den
        return carry

    lax.fori_loop(0, GH, one_head, 0)


def attend(q_own, q_par, chunks, state=None):
    shape = jax.ShapeDtypeStruct((2 * GH, PAIR, HD), F32)
    first = state is None
    n = len(chunks)
    return pl.pallas_call(
        functools.partial(attend_body, first, n),
        out_shape=(shape, shape),
        in_specs=[VMEM] * (2 + n + (0 if first else 2)),
        out_specs=(VMEM, VMEM),
        input_output_aliases={} if first else {2 + n: 0, 3 + n: 1},
        compiler_params=params(),
        cost_estimate=cost(
            2 * GH * PAIR * PAIR * n * HD * 4, 2 * 1024 * 1024, 2 * GH * PAIR * PAIR * n
        ),
        name="attend",
    )(q_own, q_par, *chunks, *(() if first else state))


def last_par_body(q_par, chunk, num_in, den_in, msg):
    keys, vals = chunk[:, :HD], chunk[:, HD:]
    lane = lax.broadcasted_iota(jnp.int32, (PAIR, HD), 1)
    plane = jnp.zeros((PAIR, HD), F32)
    for h in range(GH):
        num, den = add_keys(q_par[h], keys, vals)
        msg[h] = (num + num_in[GH + h]).astype(BF)
        den = jnp.broadcast_to(den, (PAIR, HD)) + den_in[GH + h]
        high = den.astype(BF).astype(F32)
        plane = jnp.where(lane == 2 * h, high, plane)
        plane = jnp.where(lane == 2 * h + 1, den - high, plane)
    msg[GH] = plane.astype(BF)


def last_own_body(q_own, chunk, num_in, den_in, num_out, den_out):
    keys, vals = chunk[:, :HD], chunk[:, HD:]
    for h in range(GH):
        num, den = add_keys(q_own[h], keys, vals)
        num_out[h] = num + num_in[h]
        den_out[h] = jnp.broadcast_to(den, (PAIR, HD)) + den_in[h]


def attend_last(q, chunk, state, own):
    shape = jax.ShapeDtypeStruct((GH, PAIR, HD), F32)
    message = jax.ShapeDtypeStruct((GH + 1, PAIR, HD), BF)
    return pl.pallas_call(
        last_own_body if own else last_par_body,
        out_shape=(shape, shape) if own else message,
        in_specs=[VMEM] * 4,
        out_specs=(VMEM, VMEM) if own else VMEM,
        compiler_params=params(),
        cost_estimate=cost(GH * PAIR * PAIR * HD * 4, 2 * 1024 * 1024, GH * PAIR * PAIR),
        name="attend_last",
    )(q, chunk, *state)


def merge_body(num_ref, den_ref, msg, out_own, out_oth):
    plane = msg[GH].astype(F32)
    for h in range(GH):
        den = den_ref[h][:, :1] + plane[:, 2 * h : 2 * h + 1] + plane[:, 2 * h + 1 : 2 * h + 2]
        value = ((num_ref[h] + msg[h].astype(F32)) / den).astype(BF)
        out_own[:, h * HD : (h + 1) * HD] = value[:TOK]
        out_oth[:, h * HD : (h + 1) * HD] = value[TOK:]


def merge(num, den, msg):
    shape = jax.ShapeDtypeStruct((TOK, QC), BF)
    return pl.pallas_call(
        merge_body,
        out_shape=(shape, shape),
        in_specs=[VMEM] * 3,
        out_specs=(VMEM, VMEM),
        compiler_params=params(),
        cost_estimate=cost(GH * PAIR * HD * 4, 1024 * 1024),
        name="merge",
    )(num, den, msg)


def output_body(layer, n, lead_ref, *refs):
    att, x, (w_own, w_oth, mod_ref), outs = (
        refs[: 2 * n],
        refs[2 * n : 3 * n],
        refs[3 * n : 3 * n + 3],
        refs[3 * n + 3 :],
    )
    gate = mod_ref[layer, 1, pl.ds(sample_lead(lead_ref) + layer, 1), :]
    dims = (((1,), (1,)), ((), ()))
    for part in range(n):
        update = lax.dot_general(att[2 * part][...], w_own[...], dims, preferred_element_type=F32)
        update += lax.dot_general(
            att[2 * part + 1][...], w_oth[...], dims, preferred_element_type=F32
        )
        rows = (x[part][...].astype(F32) + gate * update).astype(BF)
        outs[part][...] = rows.reshape(outs[part].shape)


def output(layer, lead, att, x, w_own, w_oth, modulation):
    n = len(x)
    return one_step(
        functools.partial(output_body, layer, n),
        lead,
        (*map(whole, att), *map(whole, x), w_own, w_oth, whole(modulation)),
        (jax.ShapeDtypeStruct((TOK, D) if n > 1 else (1, TOK, D), BF),) * n,
        [],
        2 * n * TOK * D * 2 * QC,
        "output",
    )


def after(value, *events):
    return lax.optimization_barrier((value, *events))[0]


def attention(kv, q, done_by_hop, tick):
    q_par = lax.ppermute(q, "ctx", X_SWAP)
    up = lax.ppermute(kv, "ctx", z_step(1))
    down = lax.ppermute(kv, "ctx", z_step(-1))
    waiting, state = [(kv,)], None
    for k, count in enumerate(done_by_hop):
        waiting.append((up, down))
        up = lax.ppermute(up, "ctx", z_step(1))
        down = lax.ppermute(down, "ctx", z_step(-1))
        for _ in range(count):
            state = attend(q, q_par, waiting.pop(0), state)
        if count:
            up, down, state = lax.optimization_barrier((up, down, state))
        tie = tick(k + 1, up)
        if tie is not None:
            up = after(up, tie)
    waiting.append((up, down))
    far = lax.ppermute(up, "ctx", z_step(1))
    for group in waiting:
        state = attend(q, q_par, group, state)
    msg = attend_last(q_par, far, state, False)
    got = lax.ppermute(msg, "ctx", X_SWAP)
    num, den = attend_last(q, far, after(state, msg), True)
    return merge(num, den, got)


def assemble_body(tail_qkv, tail_out, head_qkv, head_out, near_ref, tq, to, hq, ho, sems):
    copies = [
        pltpu.make_async_copy(src, dst, sems.at[i])
        for i, (src, dst) in enumerate(
            ((tail_qkv, tq), (tail_out, to), (head_qkv, hq), (head_out, ho))
        )
    ]
    for copy in copies:
        copy.start()
    for copy in copies:
        copy.wait()
    nq, nk = 2 * QC, 2 * HD
    for c in range(2):

        def keys(ref):
            return ref[:, nq + c * HD : nq + (c + 1) * HD]

        def vals(ref):
            return ref[:, nq + nk + c * HD : nq + nk + (c + 1) * HD]

        def wide(ref):
            return ref[:, c * QC : (c + 1) * QC]

        row = jnp.concatenate(
            (keys(tq), vals(tq), wide(tq)[:, : 2 * HD], wide(to), wide(tq)[:, 2 * HD :],
             wide(hq), wide(ho), keys(hq), vals(hq)), axis=1
        )
        for z in range(NZ):
            near_ref[2 * z + c] = row


def assemble(tail_qkv, tail_out, head_qkv, head_out):
    args = [
        pltpu.with_memory_space_constraint(a, pltpu.MemorySpace.HBM)
        for a in (tail_qkv, tail_out, head_qkv, head_out)
    ]
    rows = tail_qkv.shape[0]
    return pl.pallas_call(
        assemble_body,
        out_shape=jax.ShapeDtypeStruct((2 * NZ, rows, 2 * AC + 2 * QC), BF),
        in_specs=[pl.BlockSpec(memory_space=pltpu.MemorySpace.HBM)] * 4,
        out_specs=VMEM,
        scratch_shapes=[pltpu.VMEM(a.shape, a.dtype) for a in args] + [pltpu.SemaphoreType.DMA((4,))],
        compiler_params=params(),
        cost_estimate=cost(0, 1024 * 1024),
        name="assemble",
    )(*args)


def position(axis):
    if axis == "y":
        return lax.axis_index("section") // 2
    return lax.rem(lax.axis_index("section"), 2) * 2 + lax.axis_index("ctx") // 16


def place_body(axes, *refs):
    for k, axis in enumerate(axes):
        pieces, out = refs[4 * k : 4 * k + 4], refs[4 * len(axes) + k]
        at = position(axis)
        for ref, back in zip(pieces, (0, 1, 3, 2)):
            out[lax.rem(at + 4 - back, 4)] = ref[...]


def place(axes, sets):
    shapes = [jax.ShapeDtypeStruct((4, *pieces[0].shape), BF) for pieces in sets]
    return pl.pallas_call(
        functools.partial(place_body, axes),
        out_shape=tuple(shapes),
        in_specs=[VMEM] * (4 * len(sets)),
        out_specs=(VMEM,) * len(sets),
        compiler_params=params(),
        cost_estimate=cost(0, sum(8 * p[0].size for p in sets)),
        name="place",
    )(*[p for pieces in sets for p in pieces])


def ring_of_4(rows, axis, step):
    return (rows, *(lax.ppermute(rows, axis, step(by)) for by in (1, -1, 2)))


def per_device(
    latent_state, lead_step, tail_qkv, tail_out, head_qkv, head_out, modulation, qk_gain
):
    x_own = lax.ppermute(latent_state[0], "section", section_step(1))

    near = assemble(tail_qkv, tail_out, head_qkv, head_out)
    near = lax.all_to_all(near, "ctx", 0, 0, axis_index_groups=ZC_GROUPS)
    near, x_own = lax.optimization_barrier((near, x_own))
    x_oth = lax.ppermute(x_own, "ctx", CORE_SWAP)
    near = near.reshape(-1, near.shape[-1])
    half = KVC + 2 * HD
    by_x, by_y = near[:, :half], near[:, half : 2 * half]
    later = lax.all_gather(
        near[:, 2 * half :], BOTH, axis=0, tiled=True, axis_index_groups=XY_GROUPS
    )
    by_y, by_x = place(
        "yx",
        (ring_of_4(by_y, "section", y_step), ring_of_4(by_x, BOTH, x_step)),
    )
    by_y, by_x, x_oth = lax.optimization_barrier((by_y, by_x, x_oth))
    by_y, by_x = place(
        "xy",
        (
            ring_of_4(by_y.reshape(-1, half), BOTH, x_step),
            ring_of_4(by_x.reshape(-1, half), "section", y_step),
        ),
    )
    by_x = by_x.reshape(D, half)
    by_y = by_y.reshape(NX, NY, -1, half).transpose(1, 0, 2, 3).reshape(D, half)
    kv, q = project(
        0, lead_step, x_own, x_oth, [columns(by_x, HD, i) for i in range(4)] + [columns(by_y, HD, 3)],
        modulation, qk_gain,
    )
    side = {}

    def beside_tail(k, event):
        if k == 2:
            side["out"] = lax.ppermute(after(by_y, event), "ctx", CORE_SWAP)

    att_own, att_oth = attention(kv, q, (0, 2), beside_tail)
    got_oth, got_own = (lax.ppermute(a, "ctx", CORE_SWAP) for a in (att_own, att_oth))
    x_own, x_oth = output(
        0, lead_step, (att_own, got_own, att_oth, got_oth), (x_own, x_oth),
        columns(by_y, QC, 0), columns(side["out"], QC, 0), modulation,
    )

    kv, q = project(
        1, lead_step, x_own, x_oth, [columns(later, HD, i) for i in (6, 7, 0, 1, 2)], modulation, qk_gain
    )
    side["tail"] = lax.ppermute(after(x_own, q), "section", section_step(-1))

    def beside_head(k, event):
        if k == 1:
            return side["tail"]
        if k == 2:
            side["out"] = lax.ppermute(
                after(later[:, QC : 2 * QC], event), "ctx", CORE_SWAP
            )
        return None

    att_own, att_oth = attention(kv, q, (0, 2), beside_head)
    got_own = lax.ppermute(att_oth, "ctx", CORE_SWAP)
    (head_new,) = output(
        1, lead_step, (att_own, got_own), (x_own,), columns(later, QC, 1), whole(side["out"]), modulation
    )
    return (side["tail"][None], head_new)


def solution(mesh):
    in_specs = (
        P("section", "ctx", None),
        P(),
        P(BOTH, None),
        P(BOTH, None),
        P(BOTH, None),
        P(BOTH, None),
        P(),
        P(),
    )
    out_specs = (P("section", "ctx", None), P("section", "ctx", None))
    return jax.shard_map(
        per_device, mesh=mesh, in_specs=in_specs, out_specs=out_specs, check_vma=False
    )
```

```python
import functools
import math

import jax
import jax.numpy as jnp
from jax import lax
from jax.experimental import pallas as pl
from jax.experimental.pallas import tpu as pltpu
from jax.sharding import PartitionSpec as P

D = 1536
HD = 128
GH = 3
QC = GH * HD
KVC = 2 * HD
AC = KVC + QC
TOK = 160
PAIR = 2 * TOK
NZ = 8
NX = 4
NY = 4
EPS = 1e-06
EXP2_SCALE = math.log2(math.e) * HD ** (-0.5)
VMEM = pl.BlockSpec(memory_space=pltpu.VMEM)
SMEM = pl.BlockSpec(memory_space=pltpu.SMEM)
BF = jnp.bfloat16
F32 = jnp.float32


def flat_id(x, y, z, c):
    return (y * 2 + (x >> 1)) * 32 + (x & 1) * 16 + z * 2 + c


CORE_SWAP = [(i, i ^ 1) for i in range(32)]
X_SWAP = [(i, i ^ 16) for i in range(32)]
ZC_GROUPS = [[xl * 16 + i for i in range(16)] for xl in range(2)]
XY_GROUPS = [
    [flat_id(x, y, z, c) for y in range(NY) for x in range(NX)] for z in range(NZ) for c in range(2)
]
BOTH = ("section", "ctx")


def z_step(by):
    return [(i, (i & 16) | ((((i >> 1) + by) % NZ) << 1) | (i & 1)) for i in range(32)]


def x_step(by):
    return [
        (flat_id(x, y, z, c), flat_id((x + by) % NX, y, z, c))
        for x in range(NX) for y in range(NY) for z in range(NZ) for c in range(2)
    ]


def y_step(by):
    return [(i, (((i >> 1) + by) % NY) << 1 | (i & 1)) for i in range(8)]


def section_step(by):
    return [(s, (s + by) % 8) for s in range(8)]


def cost(flops, nbytes, trans=0):
    return pl.CostEstimate(flops=int(flops), bytes_accessed=int(nbytes), transcendentals=int(trans))


def params():
    return pltpu.CompilerParams(vmem_limit_bytes=12 * 1024 * 1024)


def sample_lead(lead_ref):
    return lead_ref[lax.rem(lax.axis_index("section") + 7, 8)]


def head_normal(values, gain_row):
    factor = lax.rsqrt(jnp.mean(values * values, axis=-1, keepdims=True) + EPS)
    return (values * factor * gain_row).astype(BF)


def project_body(layer, lead_ref, own_ref, oth_ref, wk_ref, wv_ref, wq0_ref, wq1_ref, wq2_ref, mod_ref, gain_ref, kv_ref, q_ref, normed):
    row = mod_ref[layer, 0, pl.ds(sample_lead(lead_ref) + layer, 1), :]
    for part, ref in enumerate((own_ref, oth_ref)):
        x = ref[...].astype(F32)
        factor = lax.rsqrt(jnp.mean(x * x, axis=-1, keepdims=True) + EPS)
        normed[part * TOK : (part + 1) * TOK, :] = (x * factor * row).astype(BF)
    keys = jnp.dot(normed[...], wk_ref[...], preferred_element_type=F32)
    kv_ref[:, :HD] = head_normal(keys, gain_ref[layer, 1:2, :])
    vals = jnp.dot(normed[...], wv_ref[...], preferred_element_type=F32)
    kv_ref[:, HD:] = vals.astype(BF)
    for h, ref in enumerate((wq0_ref, wq1_ref, wq2_ref)):
        q = jnp.dot(normed[...], ref[...], preferred_element_type=F32)
        q_ref[h] = head_normal(q, gain_ref[layer, 0:1, :])


def columns(array, width, block):
    return array, pl.BlockSpec((array.shape[0], width), lambda i: (0, block))


def whole(array):
    return array, pl.BlockSpec(array.shape, lambda i: (0,) * array.ndim)


def one_step(body, lead, operands, shapes, scratch, flops, name):
    arrays, specs = zip(*operands)
    return pl.pallas_call(
        body,
        grid=(1,),
        out_shape=shapes,
        in_specs=[SMEM, *specs],
        out_specs=tuple(
            pl.BlockSpec(s.shape, lambda i, n=len(s.shape): (0,) * n) for s in shapes
        ),
        scratch_shapes=scratch,
        compiler_params=params(),
        cost_estimate=cost(flops, 4 * 1024 * 1024),
        name=name,
    )(lead, *arrays)


def project(layer, lead, own, oth, weights, modulation, qk_gain):
    return one_step(
        functools.partial(project_body, layer),
        lead,
        (whole(own), whole(oth), *weights, whole(modulation), whole(qk_gain)),
        (
            jax.ShapeDtypeStruct((PAIR, KVC), BF),
            jax.ShapeDtypeStruct((GH, PAIR, HD), BF),
        ),
        [pltpu.VMEM((PAIR, D), BF)],
        2 * PAIR * D * AC,
        "project",
    )


def add_keys(q, keys, vals):
    scores = lax.dot_general(q, keys, (((1,), (1,)), ((), ())), preferred_element_type=F32)
    weights = jnp.exp2(scores * EXP2_SCALE)
    return (
        jnp.dot(weights.astype(BF), vals, preferred_element_type=F32),
        jnp.sum(weights, axis=-1, keepdims=True),
    )


def attend_body(first, n_chunks, *refs):
    q_own, q_par = refs[:2]
    chunks = refs[2 : 2 + n_chunks]
    rest = refs[2 + n_chunks :]
    if first:
        num_out, den_out = rest
    else:
        num_in, den_in, num_out, den_out = rest
    def one_head(h, carry):
        for side, q_ref in enumerate((q_own, q_par)):
            q = q_ref[h]
            num = den = None
            for ref in chunks:
                part, total = add_keys(q, ref[:, :HD], ref[:, HD:])
                num = part if num is None else num + part
                den = total if den is None else den + total
            den = jnp.broadcast_to(den, (PAIR, HD))
            if not first:
                num = num + num_in[side * GH + h]
                den = den + den_in[side * GH + h]
            num_out[side * GH + h] = num
            den_out[side * GH + h] = den
        return carry

    lax.fori_loop(0, GH, one_head, 0)


def attend(q_own, q_par, chunks, state=None):
    shape = jax.ShapeDtypeStruct((2 * GH, PAIR, HD), F32)
    first = state is None
    n = len(chunks)
    return pl.pallas_call(
        functools.partial(attend_body, first, n),
        out_shape=(shape, shape),
        in_specs=[VMEM] * (2 + n + (0 if first else 2)),
        out_specs=(VMEM, VMEM),
        input_output_aliases={} if first else {2 + n: 0, 3 + n: 1},
        compiler_params=params(),
        cost_estimate=cost(
            2 * GH * PAIR * PAIR * n * HD * 4, 2 * 1024 * 1024, 2 * GH * PAIR * PAIR * n
        ),
        name="attend",
    )(q_own, q_par, *chunks, *(() if first else state))


def last_par_body(q_par, chunk, num_in, den_in, msg):
    keys, vals = chunk[:, :HD], chunk[:, HD:]
    lane = lax.broadcasted_iota(jnp.int32, (PAIR, HD), 1)
    plane = jnp.zeros((PAIR, HD), F32)
    for h in range(GH):
        num, den = add_keys(q_par[h], keys, vals)
        msg[h] = (num + num_in[GH + h]).astype(BF)
        den = jnp.broadcast_to(den, (PAIR, HD)) + den_in[GH + h]
        high = den.astype(BF).astype(F32)
        plane = jnp.where(lane == 2 * h, high, plane)
        plane = jnp.where(lane == 2 * h + 1, den - high, plane)
    msg[GH] = plane.astype(BF)


def last_own_body(q_own, chunk, num_in, den_in, num_out, den_out):
    keys, vals = chunk[:, :HD], chunk[:, HD:]
    for h in range(GH):
        num, den = add_keys(q_own[h], keys, vals)
        num_out[h] = num + num_in[h]
        den_out[h] = jnp.broadcast_to(den, (PAIR, HD)) + den_in[h]


def attend_last(q, chunk, state, own):
    shape = jax.ShapeDtypeStruct((GH, PAIR, HD), F32)
    message = jax.ShapeDtypeStruct((GH + 1, PAIR, HD), BF)
    return pl.pallas_call(
        last_own_body if own else last_par_body,
        out_shape=(shape, shape) if own else message,
        in_specs=[VMEM] * 4,
        out_specs=(VMEM, VMEM) if own else VMEM,
        compiler_params=params(),
        cost_estimate=cost(GH * PAIR * PAIR * HD * 4, 2 * 1024 * 1024, GH * PAIR * PAIR),
        name="attend_last",
    )(q, chunk, *state)


def merge_body(num_ref, den_ref, msg, out_own, out_oth):
    plane = msg[GH].astype(F32)
    for h in range(GH):
        den = den_ref[h][:, :1] + plane[:, 2 * h : 2 * h + 1] + plane[:, 2 * h + 1 : 2 * h + 2]
        value = ((num_ref[h] + msg[h].astype(F32)) / den).astype(BF)
        out_own[:, h * HD : (h + 1) * HD] = value[:TOK]
        out_oth[:, h * HD : (h + 1) * HD] = value[TOK:]


def merge(num, den, msg):
    shape = jax.ShapeDtypeStruct((TOK, QC), BF)
    return pl.pallas_call(
        merge_body,
        out_shape=(shape, shape),
        in_specs=[VMEM] * 3,
        out_specs=(VMEM, VMEM),
        compiler_params=params(),
        cost_estimate=cost(GH * PAIR * HD * 4, 1024 * 1024),
        name="merge",
    )(num, den, msg)


def output_body(layer, n, lead_ref, *refs):
    att, x, (w_own, w_oth, mod_ref), outs = (
        refs[: 2 * n],
        refs[2 * n : 3 * n],
        refs[3 * n : 3 * n + 3],
        refs[3 * n + 3 :],
    )
    gate = mod_ref[layer, 1, pl.ds(sample_lead(lead_ref) + layer, 1), :]
    dims = (((1,), (1,)), ((), ()))
    for part in range(n):
        update = lax.dot_general(att[2 * part][...], w_own[...], dims, preferred_element_type=F32)
        update += lax.dot_general(
            att[2 * part + 1][...], w_oth[...], dims, preferred_element_type=F32
        )
        rows = (x[part][...].astype(F32) + gate * update).astype(BF)
        outs[part][...] = rows.reshape(outs[part].shape)


def output(layer, lead, att, x, w_own, w_oth, modulation):
    n = len(x)
    return one_step(
        functools.partial(output_body, layer, n),
        lead,
        (*map(whole, att), *map(whole, x), w_own, w_oth, whole(modulation)),
        (jax.ShapeDtypeStruct((TOK, D) if n > 1 else (1, TOK, D), BF),) * n,
        [],
        2 * n * TOK * D * 2 * QC,
        "output",
    )


def after(value, *events):
    return lax.optimization_barrier((value, *events))[0]


def attention(kv, q, done_by_hop, tick):
    q_par = lax.ppermute(q, "ctx", X_SWAP)
    up = lax.ppermute(kv, "ctx", z_step(1))
    down = lax.ppermute(kv, "ctx", z_step(-1))
    waiting, state = [(kv,)], None
    for k, count in enumerate(done_by_hop):
        waiting.append((up, down))
        up = lax.ppermute(up, "ctx", z_step(1))
        down = lax.ppermute(down, "ctx", z_step(-1))
        for _ in range(count):
            state = attend(q, q_par, waiting.pop(0), state)
        if count:
            up, down, state = lax.optimization_barrier((up, down, state))
        tie = tick(k + 1, up)
        if tie is not None:
            up = after(up, tie)
    waiting.append((up, down))
    far = lax.ppermute(up, "ctx", z_step(1))
    for group in waiting:
        state = attend(q, q_par, group, state)
    msg = attend_last(q_par, far, state, False)
    got = lax.ppermute(msg, "ctx", X_SWAP)
    num, den = attend_last(q, far, after(state, msg), True)
    return merge(num, den, got)


def assemble_body(tail_qkv, tail_out, head_qkv, head_out, near_ref, tq, to, hq, ho, sems):
    copies = [
        pltpu.make_async_copy(src, dst, sems.at[i])
        for i, (src, dst) in enumerate(
            ((tail_qkv, tq), (tail_out, to), (head_qkv, hq), (head_out, ho))
        )
    ]
    for copy in copies:
        copy.start()
    for copy in copies:
        copy.wait()
    nq, nk = 2 * QC, 2 * HD
    for c in range(2):

        def keys(ref):
            return ref[:, nq + c * HD : nq + (c + 1) * HD]

        def vals(ref):
            return ref[:, nq + nk + c * HD : nq + nk + (c + 1) * HD]

        def wide(ref):
            return ref[:, c * QC : (c + 1) * QC]

        row = jnp.concatenate(
            (keys(tq), vals(tq), wide(tq)[:, : 2 * HD], wide(to), wide(tq)[:, 2 * HD :],
             wide(hq), wide(ho), keys(hq), vals(hq)), axis=1
        )
        for z in range(NZ):
            near_ref[2 * z + c] = row


def assemble(tail_qkv, tail_out, head_qkv, head_out):
    args = [
        pltpu.with_memory_space_constraint(a, pltpu.MemorySpace.HBM)
        for a in (tail_qkv, tail_out, head_qkv, head_out)
    ]
    rows = tail_qkv.shape[0]
    return pl.pallas_call(
        assemble_body,
        out_shape=jax.ShapeDtypeStruct((2 * NZ, rows, 2 * AC + 2 * QC), BF),
        in_specs=[pl.BlockSpec(memory_space=pltpu.MemorySpace.HBM)] * 4,
        out_specs=VMEM,
        scratch_shapes=[pltpu.VMEM(a.shape, a.dtype) for a in args] + [pltpu.SemaphoreType.DMA((4,))],
        compiler_params=params(),
        cost_estimate=cost(0, 1024 * 1024),
        name="assemble",
    )(*args)


def position(axis):
    if axis == "y":
        return lax.axis_index("section") // 2
    return lax.rem(lax.axis_index("section"), 2) * 2 + lax.axis_index("ctx") // 16


def place_body(axes, *refs):
    for k, axis in enumerate(axes):
        pieces, out = refs[4 * k : 4 * k + 4], refs[4 * len(axes) + k]
        at = position(axis)
        for ref, back in zip(pieces, (0, 2, 1, 3)):
            out[lax.rem(at + 4 - back, 4)] = ref[...]


def place(axes, sets):
    shapes = [jax.ShapeDtypeStruct((4, *pieces[0].shape), BF) for pieces in sets]
    return pl.pallas_call(
        functools.partial(place_body, axes),
        out_shape=tuple(shapes),
        in_specs=[VMEM] * (4 * len(sets)),
        out_specs=(VMEM,) * len(sets),
        compiler_params=params(),
        cost_estimate=cost(0, sum(8 * p[0].size for p in sets)),
        name="place",
    )(*[p for pieces in sets for p in pieces])


def ring_of_4(rows, axis, step):
    return (rows, *(lax.ppermute(rows, axis, step(by)) for by in (2, 1, -1)))


def per_device(
    latent_state, lead_step, tail_qkv, tail_out, head_qkv, head_out, modulation, qk_gain
):
    x_own = lax.ppermute(latent_state[0], "section", section_step(1))

    near = assemble(tail_qkv, tail_out, head_qkv, head_out)
    near = lax.all_to_all(near, "ctx", 0, 0, axis_index_groups=ZC_GROUPS)
    near, x_own = lax.optimization_barrier((near, x_own))
    x_oth = lax.ppermute(x_own, "ctx", CORE_SWAP)
    near = near.reshape(-1, near.shape[-1])
    half = KVC + 2 * HD
    by_x, by_y = near[:, :half], near[:, half : 2 * half]
    later = lax.all_gather(
        near[:, 2 * half :], BOTH, axis=0, tiled=True, axis_index_groups=XY_GROUPS
    )
    by_y, by_x = place(
        "yx",
        (ring_of_4(by_y, "section", y_step), ring_of_4(by_x, BOTH, x_step)),
    )
    by_y, by_x, x_oth = lax.optimization_barrier((by_y, by_x, x_oth))
    by_y, by_x = place(
        "xy",
        (
            ring_of_4(by_y.reshape(-1, half), BOTH, x_step),
            ring_of_4(by_x.reshape(-1, half), "section", y_step),
        ),
    )
    by_x = by_x.reshape(D, half)
    by_y = by_y.reshape(NX, NY, -1, half).transpose(1, 0, 2, 3).reshape(D, half)
    kv, q = project(
        0, lead_step, x_own, x_oth, [columns(by_x, HD, i) for i in range(4)] + [columns(by_y, HD, 3)],
        modulation, qk_gain,
    )
    side = {}

    def beside_tail(k, event):
        if k == 2:
            side["out"] = lax.ppermute(after(by_y, event), "ctx", CORE_SWAP)

    att_own, att_oth = attention(kv, q, (0, 2), beside_tail)
    got_oth, got_own = (lax.ppermute(a, "ctx", CORE_SWAP) for a in (att_own, att_oth))
    x_own, x_oth = output(
        0, lead_step, (att_own, got_own, att_oth, got_oth), (x_own, x_oth),
        columns(by_y, QC, 0), columns(side["out"], QC, 0), modulation,
    )

    kv, q = project(
        1, lead_step, x_own, x_oth, [columns(later, HD, i) for i in (6, 7, 0, 1, 2)], modulation, qk_gain
    )
    side["tail"] = lax.ppermute(after(x_own, q), "section", section_step(-1))

    def beside_head(k, event):
        if k == 1:
            return side["tail"]
        if k == 2:
            side["out"] = lax.ppermute(
                after(later[:, QC : 2 * QC], event), "ctx", CORE_SWAP
            )
        return None

    att_own, att_oth = attention(kv, q, (0, 2), beside_head)
    got_own = lax.ppermute(att_oth, "ctx", CORE_SWAP)
    (head_new,) = output(
        1, lead_step, (att_own, got_own), (x_own,), columns(later, QC, 1), whole(side["out"]), modulation
    )
    return (side["tail"][None], head_new)


def solution(mesh):
    in_specs = (
        P("section", "ctx", None),
        P(),
        P(BOTH, None),
        P(BOTH, None),
        P(BOTH, None),
        P(BOTH, None),
        P(),
        P(),
    )
    out_specs = (P("section", "ctx", None), P("section", "ctx", None))
    return jax.shard_map(
        per_device, mesh=mesh, in_specs=in_specs, out_specs=out_specs, check_vma=False
    )
```

```python
import functools
import math

import jax
import jax.numpy as jnp
from jax import lax
from jax.experimental import pallas as pl
from jax.experimental.pallas import tpu as pltpu
from jax.sharding import PartitionSpec as P

D = 1536
HD = 128
GH = 3
QC = GH * HD
KVC = 2 * HD
AC = KVC + QC
TOK = 160
PAIR = 2 * TOK
NZ = 8
NX = 4
NY = 4
EPS = 1e-06
EXP2_SCALE = math.log2(math.e) * HD ** (-0.5)
VMEM = pl.BlockSpec(memory_space=pltpu.VMEM)
SMEM = pl.BlockSpec(memory_space=pltpu.SMEM)
BF = jnp.bfloat16
F32 = jnp.float32


def flat_id(x, y, z, c):
    return (y * 2 + (x >> 1)) * 32 + (x & 1) * 16 + z * 2 + c


CORE_SWAP = [(i, i ^ 1) for i in range(32)]
X_SWAP = [(i, i ^ 16) for i in range(32)]
ZC_GROUPS = [[xl * 16 + i for i in range(16)] for xl in range(2)]
XY_GROUPS = [
    [flat_id(x, y, z, c) for y in range(NY) for x in range(NX)] for z in range(NZ) for c in range(2)
]
BOTH = ("section", "ctx")


def z_step(by):
    return [(i, (i & 16) | ((((i >> 1) + by) % NZ) << 1) | (i & 1)) for i in range(32)]


def x_step(by):
    return [
        (flat_id(x, y, z, c), flat_id((x + by) % NX, y, z, c))
        for x in range(NX) for y in range(NY) for z in range(NZ) for c in range(2)
    ]


def y_step(by):
    return [(i, (((i >> 1) + by) % NY) << 1 | (i & 1)) for i in range(8)]


def section_step(by):
    return [(s, (s + by) % 8) for s in range(8)]


def cost(flops, nbytes, trans=0):
    return pl.CostEstimate(flops=int(flops), bytes_accessed=int(nbytes), transcendentals=int(trans))


def params():
    return pltpu.CompilerParams(vmem_limit_bytes=12 * 1024 * 1024)


def sample_lead(lead_ref):
    return lead_ref[lax.rem(lax.axis_index("section") + 7, 8)]


def head_normal(values, gain_row):
    factor = lax.rsqrt(jnp.mean(values * values, axis=-1, keepdims=True) + EPS)
    return (values * factor * gain_row).astype(BF)


def project_body(layer, lead_ref, own_ref, oth_ref, wk_ref, wv_ref, wq0_ref, wq1_ref, wq2_ref, mod_ref, gain_ref, kv_ref, q_ref, normed):
    row = mod_ref[layer, 0, pl.ds(sample_lead(lead_ref) + layer, 1), :]
    for part, ref in enumerate((own_ref, oth_ref)):
        x = ref[...].astype(F32)
        factor = lax.rsqrt(jnp.mean(x * x, axis=-1, keepdims=True) + EPS)
        normed[part * TOK : (part + 1) * TOK, :] = (x * factor * row).astype(BF)
    keys = jnp.dot(normed[...], wk_ref[...], preferred_element_type=F32)
    kv_ref[:, :HD] = head_normal(keys, gain_ref[layer, 1:2, :])
    vals = jnp.dot(normed[...], wv_ref[...], preferred_element_type=F32)
    kv_ref[:, HD:] = vals.astype(BF)
    for h, ref in enumerate((wq0_ref, wq1_ref, wq2_ref)):
        q = jnp.dot(normed[...], ref[...], preferred_element_type=F32)
        q_ref[h] = head_normal(q, gain_ref[layer, 0:1, :])


def columns(array, width, block):
    return array, pl.BlockSpec((array.shape[0], width), lambda i: (0, block))


def in_hbm(array):
    return pltpu.with_memory_space_constraint(array, pltpu.MemorySpace.HBM)


def whole(array):
    return array, pl.BlockSpec(array.shape, lambda i: (0,) * array.ndim)


def one_step(body, lead, operands, shapes, scratch, flops, name):
    arrays, specs = zip(*operands)
    return pl.pallas_call(
        body,
        grid=(1,),
        out_shape=shapes,
        in_specs=[SMEM, *specs],
        out_specs=tuple(
            pl.BlockSpec(s.shape, lambda i, n=len(s.shape): (0,) * n) for s in shapes
        ),
        scratch_shapes=scratch,
        compiler_params=params(),
        cost_estimate=cost(flops, 4 * 1024 * 1024),
        name=name,
    )(lead, *arrays)


def project(layer, lead, own, oth, weights, modulation, qk_gain):
    return one_step(
        functools.partial(project_body, layer),
        lead,
        (whole(own), whole(oth), *weights, whole(modulation), whole(qk_gain)),
        (
            jax.ShapeDtypeStruct((PAIR, KVC), BF),
            jax.ShapeDtypeStruct((GH, PAIR, HD), BF),
        ),
        [pltpu.VMEM((PAIR, D), BF)],
        2 * PAIR * D * AC,
        "project",
    )


def add_keys(q, keys, vals):
    scores = lax.dot_general(q, keys, (((1,), (1,)), ((), ())), preferred_element_type=F32)
    weights = jnp.exp2(scores * EXP2_SCALE)
    return (
        jnp.dot(weights.astype(BF), vals, preferred_element_type=F32),
        jnp.sum(weights, axis=-1, keepdims=True),
    )


def attend_body(first, n_chunks, *refs):
    q_own, q_par = refs[:2]
    chunks = refs[2 : 2 + n_chunks]
    rest = refs[2 + n_chunks :]
    if first:
        num_out, den_out = rest
    else:
        num_in, den_in, num_out, den_out = rest
    def one_head(h, carry):
        for side, q_ref in enumerate((q_own, q_par)):
            q = q_ref[h]
            num = den = None
            for ref in chunks:
                part, total = add_keys(q, ref[:, :HD], ref[:, HD:])
                num = part if num is None else num + part
                den = total if den is None else den + total
            den = jnp.broadcast_to(den, (PAIR, HD))
            if not first:
                num = num + num_in[side * GH + h]
                den = den + den_in[side * GH + h]
            num_out[side * GH + h] = num
            den_out[side * GH + h] = den
        return carry

    lax.fori_loop(0, GH, one_head, 0)


def attend(q_own, q_par, chunks, state=None):
    shape = jax.ShapeDtypeStruct((2 * GH, PAIR, HD), F32)
    first = state is None
    n = len(chunks)
    return pl.pallas_call(
        functools.partial(attend_body, first, n),
        out_shape=(shape, shape),
        in_specs=[VMEM] * (2 + n + (0 if first else 2)),
        out_specs=(VMEM, VMEM),
        input_output_aliases={} if first else {2 + n: 0, 3 + n: 1},
        compiler_params=params(),
        cost_estimate=cost(
            2 * GH * PAIR * PAIR * n * HD * 4, 2 * 1024 * 1024, 2 * GH * PAIR * PAIR * n
        ),
        name="attend",
    )(q_own, q_par, *chunks, *(() if first else state))


def last_par_body(q_par, chunk, num_in, den_in, msg):
    keys, vals = chunk[:, :HD], chunk[:, HD:]
    lane = lax.broadcasted_iota(jnp.int32, (PAIR, HD), 1)
    plane = jnp.zeros((PAIR, HD), F32)
    for h in range(GH):
        num, den = add_keys(q_par[h], keys, vals)
        msg[h] = (num + num_in[GH + h]).astype(BF)
        den = jnp.broadcast_to(den, (PAIR, HD)) + den_in[GH + h]
        high = den.astype(BF).astype(F32)
        plane = jnp.where(lane == 2 * h, high, plane)
        plane = jnp.where(lane == 2 * h + 1, den - high, plane)
    msg[GH] = plane.astype(BF)


def last_own_body(q_own, chunk, num_in, den_in, num_out, den_out):
    keys, vals = chunk[:, :HD], chunk[:, HD:]
    for h in range(GH):
        num, den = add_keys(q_own[h], keys, vals)
        num_out[h] = num + num_in[h]
        den_out[h] = jnp.broadcast_to(den, (PAIR, HD)) + den_in[h]


def attend_last(q, chunk, state, own):
    shape = jax.ShapeDtypeStruct((GH, PAIR, HD), F32)
    message = jax.ShapeDtypeStruct((GH + 1, PAIR, HD), BF)
    return pl.pallas_call(
        last_own_body if own else last_par_body,
        out_shape=(shape, shape) if own else message,
        in_specs=[VMEM] * 4,
        out_specs=(VMEM, VMEM) if own else VMEM,
        compiler_params=params(),
        cost_estimate=cost(GH * PAIR * PAIR * HD * 4, 2 * 1024 * 1024, GH * PAIR * PAIR),
        name="attend_last",
    )(q, chunk, *state)


def merge_body(num_ref, den_ref, msg, out_own, out_oth):
    plane = msg[GH].astype(F32)
    for h in range(GH):
        den = den_ref[h][:, :1] + plane[:, 2 * h : 2 * h + 1] + plane[:, 2 * h + 1 : 2 * h + 2]
        value = ((num_ref[h] + msg[h].astype(F32)) / den).astype(BF)
        out_own[:, h * HD : (h + 1) * HD] = value[:TOK]
        out_oth[:, h * HD : (h + 1) * HD] = value[TOK:]


def merge(num, den, msg):
    shape = jax.ShapeDtypeStruct((TOK, QC), BF)
    return pl.pallas_call(
        merge_body,
        out_shape=(shape, shape),
        in_specs=[VMEM] * 3,
        out_specs=(VMEM, VMEM),
        compiler_params=params(),
        cost_estimate=cost(GH * PAIR * HD * 4, 1024 * 1024),
        name="merge",
    )(num, den, msg)


def output_body(layer, n, lead_ref, *refs):
    att, x, (w_own, w_oth, mod_ref), outs = (
        refs[: 2 * n],
        refs[2 * n : 3 * n],
        refs[3 * n : 3 * n + 3],
        refs[3 * n + 3 :],
    )
    gate = mod_ref[layer, 1, pl.ds(sample_lead(lead_ref) + layer, 1), :]
    dims = (((1,), (1,)), ((), ()))
    for part in range(n):
        update = lax.dot_general(att[2 * part][...], w_own[...], dims, preferred_element_type=F32)
        update += lax.dot_general(
            att[2 * part + 1][...], w_oth[...], dims, preferred_element_type=F32
        )
        rows = (x[part][...].astype(F32) + gate * update).astype(BF)
        outs[part][...] = rows.reshape(outs[part].shape)


def output(layer, lead, att, x, w_own, w_oth, modulation):
    n = len(x)
    return one_step(
        functools.partial(output_body, layer, n),
        lead,
        (*map(whole, att), *map(whole, x), w_own, w_oth, whole(modulation)),
        (jax.ShapeDtypeStruct((TOK, D) if n > 1 else (1, TOK, D), BF),) * n,
        [],
        2 * n * TOK * D * 2 * QC,
        "output",
    )


def after(value, *events):
    return lax.optimization_barrier((value, *events))[0]


def attention(kv, q, done_by_hop, tick):
    q_par = lax.ppermute(q, "ctx", X_SWAP)
    up = lax.ppermute(kv, "ctx", z_step(1))
    down = lax.ppermute(kv, "ctx", z_step(-1))
    waiting, state = [(kv,)], None
    for k, count in enumerate(done_by_hop):
        waiting.append((up, down))
        up = lax.ppermute(up, "ctx", z_step(1))
        down = lax.ppermute(down, "ctx", z_step(-1))
        for _ in range(count):
            state = attend(q, q_par, waiting.pop(0), state)
        if count:
            up, down, state = lax.optimization_barrier((up, down, state))
        tie = tick(k + 1, up)
        if tie is not None:
            up = after(up, tie)
    waiting.append((up, down))
    far = lax.ppermute(up, "ctx", z_step(1))
    for group in waiting:
        state = attend(q, q_par, group, state)
    msg = attend_last(q_par, far, state, False)
    got = lax.ppermute(msg, "ctx", X_SWAP)
    num, den = attend_last(q, far, after(state, msg), True)
    return merge(num, den, got)


def assemble_body(tail_qkv, tail_out, head_qkv, head_out, near_ref, tq, to, hq, ho, sems):
    copies = [
        pltpu.make_async_copy(src, dst, sems.at[i])
        for i, (src, dst) in enumerate(
            ((tail_qkv, tq), (tail_out, to), (head_qkv, hq), (head_out, ho))
        )
    ]
    for copy in copies:
        copy.start()
    for copy in copies:
        copy.wait()
    nq, nk = 2 * QC, 2 * HD
    for c in range(2):

        def keys(ref):
            return ref[:, nq + c * HD : nq + (c + 1) * HD]

        def vals(ref):
            return ref[:, nq + nk + c * HD : nq + nk + (c + 1) * HD]

        def wide(ref):
            return ref[:, c * QC : (c + 1) * QC]

        row = jnp.concatenate(
            (keys(tq), vals(tq), wide(tq)[:, : 2 * HD], wide(to), wide(tq)[:, 2 * HD :],
             wide(hq), wide(ho), keys(hq), vals(hq)), axis=1
        )
        for z in range(NZ):
            near_ref[2 * z + c] = row


def assemble(tail_qkv, tail_out, head_qkv, head_out):
    args = [
        pltpu.with_memory_space_constraint(a, pltpu.MemorySpace.HBM)
        for a in (tail_qkv, tail_out, head_qkv, head_out)
    ]
    rows = tail_qkv.shape[0]
    return pl.pallas_call(
        assemble_body,
        out_shape=jax.ShapeDtypeStruct((2 * NZ, rows, 2 * AC + 2 * QC), BF),
        in_specs=[pl.BlockSpec(memory_space=pltpu.MemorySpace.HBM)] * 4,
        out_specs=VMEM,
        scratch_shapes=[pltpu.VMEM(a.shape, a.dtype) for a in args] + [pltpu.SemaphoreType.DMA((4,))],
        compiler_params=params(),
        cost_estimate=cost(0, 1024 * 1024),
        name="assemble",
    )(*args)


def position(axis):
    if axis == "y":
        return lax.axis_index("section") // 2
    return lax.rem(lax.axis_index("section"), 2) * 2 + lax.axis_index("ctx") // 16


def place_body(axes, *refs):
    for k, axis in enumerate(axes):
        pieces, out = refs[4 * k : 4 * k + 4], refs[4 * len(axes) + k]
        at = position(axis)
        for ref, back in zip(pieces, (0, 2, 1, 3)):
            out[lax.rem(at + 4 - back, 4)] = ref[...]


def place(axes, sets):
    shapes = [jax.ShapeDtypeStruct((4, *pieces[0].shape), BF) for pieces in sets]
    return pl.pallas_call(
        functools.partial(place_body, axes),
        out_shape=tuple(shapes),
        in_specs=[VMEM] * (4 * len(sets)),
        out_specs=(VMEM,) * len(sets),
        compiler_params=params(),
        cost_estimate=cost(0, sum(8 * p[0].size for p in sets)),
        name="place",
    )(*[p for pieces in sets for p in pieces])


def ring_of_4(rows, axis, step):
    return (rows, *(lax.ppermute(rows, axis, step(by)) for by in (2, 1, -1)))


def per_device(
    latent_state, lead_step, tail_qkv, tail_out, head_qkv, head_out, modulation, qk_gain
):
    x_own = lax.ppermute(latent_state[0], "section", section_step(1))

    near = assemble(tail_qkv, tail_out, head_qkv, head_out)
    near = lax.all_to_all(near, "ctx", 0, 0, axis_index_groups=ZC_GROUPS)
    near, x_own = lax.optimization_barrier((near, x_own))
    x_oth = lax.ppermute(x_own, "ctx", CORE_SWAP)
    near = near.reshape(-1, near.shape[-1])
    half = KVC + 2 * HD
    by_x, by_y = near[:, :half], near[:, half : 2 * half]
    later = lax.all_gather(
        near[:, 2 * half :], BOTH, axis=0, tiled=True, axis_index_groups=XY_GROUPS
    )
    by_y, by_x = place(
        "yx",
        (ring_of_4(by_y, "section", y_step), ring_of_4(by_x, BOTH, x_step)),
    )
    by_y, by_x, x_oth = lax.optimization_barrier((by_y, by_x, x_oth))
    by_y, by_x = place(
        "xy",
        (
            ring_of_4(by_y.reshape(-1, half), BOTH, x_step),
            ring_of_4(by_x.reshape(-1, half), "section", y_step),
        ),
    )
    by_x = by_x.reshape(D, half)
    by_y = by_y.reshape(NX, NY, -1, half).transpose(1, 0, 2, 3).reshape(D, half)
    kv, q = project(
        0, lead_step, x_own, x_oth, [columns(by_x, HD, i) for i in range(4)] + [columns(by_y, HD, 3)],
        modulation, qk_gain,
    )
    side = {}

    def beside_tail(k, event):
        if k == 2:
            side["out"] = lax.ppermute(after(by_y, event), "ctx", CORE_SWAP)

    att_own, att_oth = attention(kv, q, (0, 2), beside_tail)
    got_oth, got_own = (lax.ppermute(a, "ctx", CORE_SWAP) for a in (att_own, att_oth))
    x_own, x_oth = output(
        0, lead_step, (att_own, got_own, att_oth, got_oth), (x_own, x_oth),
        columns(by_y, QC, 0), columns(side["out"], QC, 0), modulation,
    )

    kv, q = project(
        1, lead_step, x_own, x_oth, [columns(in_hbm(later), HD, i) for i in (6, 7, 0, 1, 2)], modulation, qk_gain
    )
    side["tail"] = lax.ppermute(after(x_own, q), "section", section_step(-1))

    def beside_head(k, event):
        if k == 1:
            return side["tail"]
        if k == 2:
            side["out"] = lax.ppermute(
                after(later[:, QC : 2 * QC], event), "ctx", CORE_SWAP
            )
        return None

    att_own, att_oth = attention(kv, q, (0, 2), beside_head)
    got_own = lax.ppermute(att_oth, "ctx", CORE_SWAP)
    (head_new,) = output(
        1, lead_step, (att_own, got_own), (x_own,), columns(in_hbm(later), QC, 1), whole(side["out"]), modulation
    )
    return (side["tail"][None], head_new)


def solution(mesh):
    in_specs = (
        P("section", "ctx", None),
        P(),
        P(BOTH, None),
        P(BOTH, None),
        P(BOTH, None),
        P(BOTH, None),
        P(),
        P(),
    )
    out_specs = (P("section", "ctx", None), P("section", "ctx", None))
    return jax.shard_map(
        per_device, mesh=mesh, in_specs=in_specs, out_specs=out_specs, check_vma=False
    )
```

```python
import functools
import math

import jax
import jax.numpy as jnp
from jax import lax
from jax.experimental import pallas as pl
from jax.experimental.pallas import tpu as pltpu
from jax.sharding import PartitionSpec as P

D = 1536
HD = 128
GH = 3
QC = GH * HD
KVC = 2 * HD
AC = KVC + QC
TOK = 160
PAIR = 2 * TOK
NZ = 8
NX = 4
NY = 4
EPS = 1e-06
EXP2_SCALE = math.log2(math.e) * HD ** (-0.5)
VMEM = pl.BlockSpec(memory_space=pltpu.VMEM)
SMEM = pl.BlockSpec(memory_space=pltpu.SMEM)
BF = jnp.bfloat16
F32 = jnp.float32


def flat_id(x, y, z, c):
    return (y * 2 + (x >> 1)) * 32 + (x & 1) * 16 + z * 2 + c


CORE_SWAP = [(i, i ^ 1) for i in range(32)]
X_SWAP = [(i, i ^ 16) for i in range(32)]
ZC_GROUPS = [[xl * 16 + i for i in range(16)] for xl in range(2)]
XY_GROUPS = [
    [flat_id(x, y, z, c) for y in range(NY) for x in range(NX)] for z in range(NZ) for c in range(2)
]
BOTH = ("section", "ctx")


def z_step(by):
    return [(i, (i & 16) | ((((i >> 1) + by) % NZ) << 1) | (i & 1)) for i in range(32)]


def x_step(by):
    return [
        (flat_id(x, y, z, c), flat_id((x + by) % NX, y, z, c))
        for x in range(NX) for y in range(NY) for z in range(NZ) for c in range(2)
    ]


def y_step(by):
    return [(i, (((i >> 1) + by) % NY) << 1 | (i & 1)) for i in range(8)]


def section_step(by):
    return [(s, (s + by) % 8) for s in range(8)]


def cost(flops, nbytes, trans=0):
    return pl.CostEstimate(flops=int(flops), bytes_accessed=int(nbytes), transcendentals=int(trans))


def params():
    return pltpu.CompilerParams(vmem_limit_bytes=12 * 1024 * 1024)


def sample_lead(lead_ref):
    return lead_ref[lax.rem(lax.axis_index("section") + 7, 8)]


def head_normal(values, gain_row):
    factor = lax.rsqrt(jnp.mean(values * values, axis=-1, keepdims=True) + EPS)
    return (values * factor * gain_row).astype(BF)


def project_body(layer, lead_ref, own_ref, oth_ref, wk_ref, wv_ref, wq0_ref, wq1_ref, wq2_ref, mod_ref, gain_ref, kv_ref, q_ref, normed):
    row = mod_ref[layer, 0, pl.ds(sample_lead(lead_ref) + layer, 1), :]
    for part, ref in enumerate((own_ref, oth_ref)):
        x = ref[...].astype(F32)
        factor = lax.rsqrt(jnp.mean(x * x, axis=-1, keepdims=True) + EPS)
        normed[part * TOK : (part + 1) * TOK, :] = (x * factor * row).astype(BF)
    keys = jnp.dot(normed[...], wk_ref[...], preferred_element_type=F32)
    kv_ref[:, :HD] = head_normal(keys, gain_ref[layer, 1:2, :])
    vals = jnp.dot(normed[...], wv_ref[...], preferred_element_type=F32)
    kv_ref[:, HD:] = vals.astype(BF)
    for h, ref in enumerate((wq0_ref, wq1_ref, wq2_ref)):
        q = jnp.dot(normed[...], ref[...], preferred_element_type=F32)
        q_ref[h] = head_normal(q, gain_ref[layer, 0:1, :])


def columns(array, width, block):
    return array, pl.BlockSpec((array.shape[0], width), lambda i: (0, block))


def in_hbm(array):
    return pltpu.with_memory_space_constraint(array, pltpu.MemorySpace.HBM)


def whole(array):
    return array, pl.BlockSpec(array.shape, lambda i: (0,) * array.ndim)


def one_step(body, lead, operands, shapes, scratch, flops, name):
    arrays, specs = zip(*operands)
    return pl.pallas_call(
        body,
        grid=(1,),
        out_shape=shapes,
        in_specs=[SMEM, *specs],
        out_specs=tuple(
            pl.BlockSpec(s.shape, lambda i, n=len(s.shape): (0,) * n) for s in shapes
        ),
        scratch_shapes=scratch,
        compiler_params=params(),
        cost_estimate=cost(flops, 4 * 1024 * 1024),
        name=name,
    )(lead, *arrays)


def project(layer, lead, own, oth, weights, modulation, qk_gain):
    return one_step(
        functools.partial(project_body, layer),
        lead,
        (whole(own), whole(oth), *weights, whole(modulation), whole(qk_gain)),
        (
            jax.ShapeDtypeStruct((PAIR, KVC), BF),
            jax.ShapeDtypeStruct((GH, PAIR, HD), BF),
        ),
        [pltpu.VMEM((PAIR, D), BF)],
        2 * PAIR * D * AC,
        "project",
    )


def add_keys(q, keys, vals):
    scores = lax.dot_general(q, keys, (((1,), (1,)), ((), ())), preferred_element_type=F32)
    weights = jnp.exp2(scores * EXP2_SCALE)
    return (
        jnp.dot(weights.astype(BF), vals, preferred_element_type=F32),
        jnp.sum(weights, axis=-1, keepdims=True),
    )


def attend_body(first, n_chunks, *refs):
    q_own, q_par = refs[:2]
    chunks = refs[2 : 2 + n_chunks]
    rest = refs[2 + n_chunks :]
    if first:
        num_out, den_out = rest
    else:
        num_in, den_in, num_out, den_out = rest
    def one_head(h, carry):
        for side, q_ref in enumerate((q_own, q_par)):
            q = q_ref[h]
            num = den = None
            for ref in chunks:
                part, total = add_keys(q, ref[:, :HD], ref[:, HD:])
                num = part if num is None else num + part
                den = total if den is None else den + total
            den = jnp.broadcast_to(den, (PAIR, HD))
            if not first:
                num = num + num_in[side * GH + h]
                den = den + den_in[side * GH + h]
            num_out[side * GH + h] = num
            den_out[side * GH + h] = den
        return carry

    lax.fori_loop(0, GH, one_head, 0)


def attend(q_own, q_par, chunks, state=None):
    shape = jax.ShapeDtypeStruct((2 * GH, PAIR, HD), F32)
    first = state is None
    n = len(chunks)
    return pl.pallas_call(
        functools.partial(attend_body, first, n),
        out_shape=(shape, shape),
        in_specs=[VMEM] * (2 + n + (0 if first else 2)),
        out_specs=(VMEM, VMEM),
        input_output_aliases={} if first else {2 + n: 0, 3 + n: 1},
        compiler_params=params(),
        cost_estimate=cost(
            2 * GH * PAIR * PAIR * n * HD * 4, 2 * 1024 * 1024, 2 * GH * PAIR * PAIR * n
        ),
        name="attend",
    )(q_own, q_par, *chunks, *(() if first else state))


def last_par_body(q_par, chunk, num_in, den_in, msg):
    keys, vals = chunk[:, :HD], chunk[:, HD:]
    lane = lax.broadcasted_iota(jnp.int32, (PAIR, HD), 1)
    plane = jnp.zeros((PAIR, HD), F32)
    for h in range(GH):
        num, den = add_keys(q_par[h], keys, vals)
        msg[h] = (num + num_in[GH + h]).astype(BF)
        den = jnp.broadcast_to(den, (PAIR, HD)) + den_in[GH + h]
        high = den.astype(BF).astype(F32)
        plane = jnp.where(lane == 2 * h, high, plane)
        plane = jnp.where(lane == 2 * h + 1, den - high, plane)
    msg[GH] = plane.astype(BF)


def last_own_body(q_own, chunk, num_in, den_in, num_out, den_out):
    keys, vals = chunk[:, :HD], chunk[:, HD:]
    for h in range(GH):
        num, den = add_keys(q_own[h], keys, vals)
        num_out[h] = num + num_in[h]
        den_out[h] = jnp.broadcast_to(den, (PAIR, HD)) + den_in[h]


def attend_last(q, chunk, state, own):
    shape = jax.ShapeDtypeStruct((GH, PAIR, HD), F32)
    message = jax.ShapeDtypeStruct((GH + 1, PAIR, HD), BF)
    return pl.pallas_call(
        last_own_body if own else last_par_body,
        out_shape=(shape, shape) if own else message,
        in_specs=[VMEM] * 4,
        out_specs=(VMEM, VMEM) if own else VMEM,
        compiler_params=params(),
        cost_estimate=cost(GH * PAIR * PAIR * HD * 4, 2 * 1024 * 1024, GH * PAIR * PAIR),
        name="attend_last",
    )(q, chunk, *state)


def merge_body(num_ref, den_ref, msg, out_own, out_oth):
    plane = msg[GH].astype(F32)
    for h in range(GH):
        den = den_ref[h][:, :1] + plane[:, 2 * h : 2 * h + 1] + plane[:, 2 * h + 1 : 2 * h + 2]
        value = ((num_ref[h] + msg[h].astype(F32)) / den).astype(BF)
        out_own[:, h * HD : (h + 1) * HD] = value[:TOK]
        out_oth[:, h * HD : (h + 1) * HD] = value[TOK:]


def merge(num, den, msg):
    shape = jax.ShapeDtypeStruct((TOK, QC), BF)
    return pl.pallas_call(
        merge_body,
        out_shape=(shape, shape),
        in_specs=[VMEM] * 3,
        out_specs=(VMEM, VMEM),
        compiler_params=params(),
        cost_estimate=cost(GH * PAIR * HD * 4, 1024 * 1024),
        name="merge",
    )(num, den, msg)


def output_body(layer, n, lead_ref, *refs):
    att, x, (w_own, w_oth, mod_ref), outs = (
        refs[: 2 * n],
        refs[2 * n : 3 * n],
        refs[3 * n : 3 * n + 3],
        refs[3 * n + 3 :],
    )
    gate = mod_ref[layer, 1, pl.ds(sample_lead(lead_ref) + layer, 1), :]
    dims = (((1,), (1,)), ((), ()))
    for part in range(n):
        update = lax.dot_general(att[2 * part][...], w_own[...], dims, preferred_element_type=F32)
        update += lax.dot_general(
            att[2 * part + 1][...], w_oth[...], dims, preferred_element_type=F32
        )
        rows = (x[part][...].astype(F32) + gate * update).astype(BF)
        outs[part][...] = rows.reshape(outs[part].shape)


def output(layer, lead, att, x, w_own, w_oth, modulation):
    n = len(x)
    return one_step(
        functools.partial(output_body, layer, n),
        lead,
        (*map(whole, att), *map(whole, x), w_own, w_oth, whole(modulation)),
        (jax.ShapeDtypeStruct((TOK, D) if n > 1 else (1, TOK, D), BF),) * n,
        [],
        2 * n * TOK * D * 2 * QC,
        "output",
    )


def after(value, *events):
    return lax.optimization_barrier((value, *events))[0]


def attention(kv, q, done_by_hop, tick):
    q_par = lax.ppermute(q, "ctx", X_SWAP)
    up = lax.ppermute(kv, "ctx", z_step(1))
    down = lax.ppermute(kv, "ctx", z_step(-1))
    waiting, state = [(kv,)], None
    for k, count in enumerate(done_by_hop):
        waiting.append((up, down))
        up = lax.ppermute(up, "ctx", z_step(1))
        down = lax.ppermute(down, "ctx", z_step(-1))
        for _ in range(count):
            state = attend(q, q_par, waiting.pop(0), state)
        if count:
            up, down, state = lax.optimization_barrier((up, down, state))
        tie = tick(k + 1, up)
        if tie is not None:
            up = after(up, tie)
    waiting.append((up, down))
    far = lax.ppermute(up, "ctx", z_step(1))
    for group in waiting:
        state = attend(q, q_par, group, state)
    msg = attend_last(q_par, far, state, False)
    got = lax.ppermute(msg, "ctx", X_SWAP)
    num, den = attend_last(q, far, after(state, msg), True)
    return merge(num, den, got)


def assemble_body(tail_qkv, tail_out, head_qkv, head_out, near_ref, tq, to, hq, ho, sems):
    copies = [
        pltpu.make_async_copy(src, dst, sems.at[i])
        for i, (src, dst) in enumerate(
            ((tail_qkv, tq), (tail_out, to), (head_qkv, hq), (head_out, ho))
        )
    ]
    for copy in copies:
        copy.start()
    for copy in copies:
        copy.wait()
    nq, nk = 2 * QC, 2 * HD
    for c in range(2):

        def keys(ref):
            return ref[:, nq + c * HD : nq + (c + 1) * HD]

        def vals(ref):
            return ref[:, nq + nk + c * HD : nq + nk + (c + 1) * HD]

        def wide(ref):
            return ref[:, c * QC : (c + 1) * QC]

        row = jnp.concatenate(
            (keys(tq), vals(tq), wide(tq)[:, : 2 * HD], wide(to), wide(tq)[:, 2 * HD :],
             wide(hq), wide(ho), keys(hq), vals(hq)), axis=1
        )
        for z in range(NZ):
            near_ref[2 * z + c] = row


def assemble(tail_qkv, tail_out, head_qkv, head_out):
    args = [
        pltpu.with_memory_space_constraint(a, pltpu.MemorySpace.HBM)
        for a in (tail_qkv, tail_out, head_qkv, head_out)
    ]
    rows = tail_qkv.shape[0]
    return pl.pallas_call(
        assemble_body,
        out_shape=jax.ShapeDtypeStruct((2 * NZ, rows, 2 * AC + 2 * QC), BF),
        in_specs=[pl.BlockSpec(memory_space=pltpu.MemorySpace.HBM)] * 4,
        out_specs=VMEM,
        scratch_shapes=[pltpu.VMEM(a.shape, a.dtype) for a in args] + [pltpu.SemaphoreType.DMA((4,))],
        compiler_params=params(),
        cost_estimate=cost(0, 1024 * 1024),
        name="assemble",
    )(*args)


def position(axis):
    if axis == "y":
        return lax.axis_index("section") // 2
    return lax.rem(lax.axis_index("section"), 2) * 2 + lax.axis_index("ctx") // 16


def place_body(axes, *refs):
    for k, axis in enumerate(axes):
        n = len(axes)
        pieces, out = refs[k : 4 * n : n], refs[4 * n + k]
        at = position(axis)
        for ref, back in zip(pieces, (0, 2, 1, 3)):
            out[lax.rem(at + 4 - back, 4)] = ref[...]


def place(axes, sets):
    shapes = [jax.ShapeDtypeStruct((4, *pieces[0].shape), BF) for pieces in sets]
    return pl.pallas_call(
        functools.partial(place_body, axes),
        out_shape=tuple(shapes),
        in_specs=[VMEM] * (4 * len(sets)),
        out_specs=(VMEM,) * len(sets),
        compiler_params=params(),
        cost_estimate=cost(0, sum(8 * p[0].size for p in sets)),
        name="place",
    )(*[p for turn in zip(*sets) for p in turn])


def rings_of_4(*sets):
    pieces = [[rows] for rows, _, _ in sets]
    for by in (2, 1, -1):
        for got, (rows, axis, step) in zip(pieces, sets):
            got.append(lax.ppermute(rows, axis, step(by)))
    return pieces


def per_device(
    latent_state, lead_step, tail_qkv, tail_out, head_qkv, head_out, modulation, qk_gain
):
    x_own = lax.ppermute(latent_state[0], "section", section_step(1))

    near = assemble(tail_qkv, tail_out, head_qkv, head_out)
    near = lax.all_to_all(near, "ctx", 0, 0, axis_index_groups=ZC_GROUPS)
    near, x_own = lax.optimization_barrier((near, x_own))
    x_oth = lax.ppermute(x_own, "ctx", CORE_SWAP)
    near = near.reshape(-1, near.shape[-1])
    half = KVC + 2 * HD
    by_x, by_y = near[:, :half], near[:, half : 2 * half]
    later = lax.all_gather(
        near[:, 2 * half :], BOTH, axis=0, tiled=True, axis_index_groups=XY_GROUPS
    )
    by_y, by_x = place(
        "yx",
        rings_of_4((by_y, "section", y_step), (by_x, BOTH, x_step)),
    )
    by_y, by_x, x_oth = lax.optimization_barrier((by_y, by_x, x_oth))
    by_y, by_x = place(
        "xy",
        rings_of_4(
            (by_y.reshape(-1, half), BOTH, x_step), (by_x.reshape(-1, half), "section", y_step)
        ),
    )
    by_x = by_x.reshape(D, half)
    by_y = by_y.reshape(NX, NY, -1, half).transpose(1, 0, 2, 3).reshape(D, half)
    kv, q = project(
        0, lead_step, x_own, x_oth, [columns(by_x, HD, i) for i in range(4)] + [columns(by_y, HD, 3)],
        modulation, qk_gain,
    )
    side = {}

    def beside_tail(k, event):
        if k == 2:
            side["out"] = lax.ppermute(after(by_y, event), "ctx", CORE_SWAP)

    att_own, att_oth = attention(kv, q, (0, 2), beside_tail)
    got_oth, got_own = (lax.ppermute(a, "ctx", CORE_SWAP) for a in (att_own, att_oth))
    x_own, x_oth = output(
        0, lead_step, (att_own, got_own, att_oth, got_oth), (x_own, x_oth),
        columns(by_y, QC, 0), columns(side["out"], QC, 0), modulation,
    )

    kv, q = project(
        1, lead_step, x_own, x_oth, [columns(in_hbm(later), HD, i) for i in (6, 7, 0, 1, 2)], modulation, qk_gain
    )
    side["tail"] = lax.ppermute(after(x_own, q), "section", section_step(-1))

    def beside_head(k, event):
        if k == 1:
            return side["tail"]
        if k == 2:
            side["own"] = after(later[:, QC : 2 * QC], event)
            side["out"] = lax.ppermute(side["own"], "ctx", CORE_SWAP)
        return None

    att_own, att_oth = attention(kv, q, (0, 2), beside_head)
    got_own = lax.ppermute(att_oth, "ctx", CORE_SWAP)
    (head_new,) = output(
        1, lead_step, (att_own, got_own), (x_own,), whole(side["own"]), whole(side["out"]), modulation
    )
    return (side["tail"][None], head_new)


def solution(mesh):
    in_specs = (
        P("section", "ctx", None),
        P(),
        P(BOTH, None),
        P(BOTH, None),
        P(BOTH, None),
        P(BOTH, None),
        P(),
        P(),
    )
    out_specs = (P("section", "ctx", None), P("section", "ctx", None))
    return jax.shard_map(
        per_device, mesh=mesh, in_specs=in_specs, out_specs=out_specs, check_vma=False
    )
```
